512 devices in a mesh: blk: 16 (over x_hi, y), head: 32 (over z, x_lo, core).
Axes of the slice: x: 4 (x_hi: 2, x_lo: 2; x = x_hi * 2 + x_lo), y: 8, z: 8, core: 2. Of those that a mesh axis runs over, the one named last changes fastest.
Arguments:
- queries: bfloat16 [65536, 4096], P(('blk', 'head')), may hold values from -14 to 14
- keys: bfloat16 [65536, 4096], P(('blk', 'head')), may hold values from -14 to 14
- values: bfloat16 [65536, 4096], P(('blk', 'head')), may hold values from -15 to 15
- key_blocks: int32 [128, 6], replicated, may hold values from 0 to 127, as said below
- counts: int32 [128], replicated, may hold values from 3 to 6, as said below
Outputs:
- attended: bfloat16 [65536, 4096], P(('blk', 'head'))
The draws below stay inside these ranges and needn't reach their ends.
Inputs may be any that keep to these rules, and one draw needn't show every extreme that they name: `key_blocks`: row b lists, in slots below counts[b], distinct key blocks that lie in the cycle shard of b (shard = block // 8) or in one of the two shards beside it on the closed cycle of 16 shards; slots 0, 1, 2 hold b, b - 1 and b + 1 modulo 128; unused slots repeat slot 0. `counts`: some row uses all 6 slots and some row uses 3.
All inputs are finite; a program needn't handle non-finite values.
Results may differ from the reference program's by a relative error of at most 0.0036.
Values may be sent and summed in bfloat16 or wider, within the bound.
No kernel may reach another device: no remote copies, remote signals or barrier semaphores. Data moves between devices by JAX's collectives and lax.ppermute only.
A program may use at most 64 MiB of HBM per device.

```python
import jax
import jax.numpy as jnp
from jax import lax

HEADS = 32
HD = 128
D = 4096
BLOCK = 512
MAXB = 6
SHARD_BLOCKS = 8
QBLOCKS = 128
TOKENS = 65536


def draw_queries(key, part):
    base = 2.0 * jnp.clip(jax.random.normal(jax.random.fold_in(key, 1), (TOKENS, D), jnp.float32), -4.0, 4.0)
    return base.astype(jnp.bfloat16)


def draw_keys(key, part):
    base = jnp.clip(jax.random.normal(jax.random.fold_in(key, 2), (TOKENS, D), jnp.float32), -5.0, 5.0)
    return base.astype(jnp.bfloat16)


def block_pattern(key):
    span = 3 * SHARD_BLOCKS
    rows = jnp.arange(QBLOCKS, dtype=jnp.int32)
    local = rows % SHARD_BLOCKS
    shard = rows // SHARD_BLOCKS
    offsets = jnp.arange(span, dtype=jnp.int32)
    row_keys = jax.random.split(jax.random.fold_in(key, 7), QBLOCKS)
    shuffled = jax.vmap(lambda row_key: jax.random.permutation(row_key, span))(row_keys)
    ranking = jnp.argsort(shuffled, axis=1).astype(jnp.int32)
    centre = SHARD_BLOCKS + local
    inside = (offsets[None, :] >= centre[:, None] - 1) & (offsets[None, :] <= centre[:, None] + 1)
    ordering = inside.astype(jnp.int32) * span + ranking
    strides = jnp.argsort(ordering, axis=1, stable=True)[:, :MAXB - 3].astype(jnp.int32)
    picked = jnp.concatenate([centre[:, None], centre[:, None] - 1, centre[:, None] + 1, strides], axis=1)
    global_blocks = jnp.mod(shard[:, None] * SHARD_BLOCKS - SHARD_BLOCKS + picked, QBLOCKS)
    amount = 3 + jax.random.randint(jax.random.fold_in(key, 9), (QBLOCKS,), 0, MAXB - 2)
    amount = amount.at[0].set(MAXB).at[QBLOCKS - 1].set(3)
    slot_ids = jnp.arange(MAXB, dtype=jnp.int32)
    global_blocks = jnp.where(slot_ids[None, :] < amount[:, None], global_blocks, global_blocks[:, :1])
    return (global_blocks.astype(jnp.int32), amount.astype(jnp.int32))


def draw_key_blocks(key, part):
    return block_pattern(jax.random.fold_in(key, 5))[0]


def draw_counts(key, part):
    return block_pattern(jax.random.fold_in(key, 5))[1]


def block_scale(key, dims, shards, smallest, top_value):
    level, own = 1.0, jax.random.fold_in(key, 6)
    for dim, blocks in shards:
        heights = jnp.exp(jax.random.uniform(jax.random.fold_in(own, dim), (blocks,), jnp.float32, smallest / len(shards), top_value / len(shards)))
        level = level * jnp.repeat(heights, dims[dim] // blocks).reshape([-1 if axis == dim else 1 for axis in range(len(dims))])
    return level


def scatter_about(key, extent, scale, bound, pieces=(), held_as=jnp.bfloat16):
    array = scale * jax.random.normal(key, extent, jnp.float32)
    if pieces:
        array = array * block_scale(key, extent, pieces, -0.22, 0.18)
    return jnp.clip(array, -bound, bound).astype(held_as)


def setup_inputs(seed: int = 0) -> dict:
    splits = jax.random.split(jax.random.key(seed), 6)
    queries = draw_queries(jax.random.fold_in(splits[5], 71), 0)
    keys = draw_keys(jax.random.fold_in(splits[5], 71), 0)
    values = scatter_about(splits[2], (TOKENS, D), 3.0, 15.0, ((0, 512),))
    key_blocks = draw_key_blocks(jax.random.fold_in(splits[5], 71), 0)
    counts = draw_counts(jax.random.fold_in(splits[5], 71), 0)
    return {"queries": queries, "keys": keys, "values": values, "key_blocks": key_blocks, "counts": counts}


def reference(queries, keys, values, key_blocks, counts):
    scale = HD ** -0.5
    q_blocks = queries.reshape(QBLOCKS, BLOCK, HEADS, HD)
    k_blocks = keys.reshape(QBLOCKS, BLOCK, HEADS, HD)
    v_blocks = values.reshape(QBLOCKS, BLOCK, HEADS, HD)
    slot_ids = jnp.arange(MAXB, dtype=jnp.int32)

    def attend_block(index):
        listed = key_blocks[index]
        usable = (slot_ids < counts[index])[None, None, :, None]
        query_f = q_blocks[index].astype(jnp.float32)
        key_f = k_blocks[listed].astype(jnp.float32)
        value_f = v_blocks[listed].astype(jnp.float32)
        scores = jnp.einsum('qhd,jkhd->hqjk', query_f, key_f) * scale
        top = jnp.max(jnp.where(usable, scores, -jnp.inf), axis=(2, 3), keepdims=True)
        expo = jnp.where(usable, jnp.exp(scores - top), 0.0)
        total = jnp.sum(expo, axis=(2, 3))
        weights = lax.optimization_barrier(expo.astype(jnp.bfloat16)).astype(jnp.float32)
        mixed = jnp.einsum('hqjk,jkhd->qhd', weights, value_f) / jnp.transpose(total)[:, :, None]
        return mixed.astype(jnp.bfloat16).reshape(BLOCK, D)

    result = lax.map(attend_block, jnp.arange(QBLOCKS, dtype=jnp.int32))
    return result.reshape(TOKENS, D)
```

```python
import functools

import jax
import jax.numpy as jnp
from jax import lax
from jax.experimental import pallas as pl
from jax.experimental.pallas import tpu as pltpu
from jax.sharding import PartitionSpec as P

HD = 128
BLOCK = 512
MAXB = 6


def from_behind(value, axis, steps):
    count = lax.axis_size(axis)
    pairs = [(source, (source + steps) % count) for source in range(count)]
    return lax.ppermute(value, axis, pairs)


def attention_kernel(idx_ref, cnt_ref, q_ref, kp, ko, kn, vp, vo, vn, o_ref,
                     k_scr, v_scr, s_scr, m_scr, l_scr, acc_scr, sem, *, shard_rows):
    b = pl.program_id(0)

    @pl.when(b == 0)
    def _load_context():
        copies = []
        for i, (src, dst, part) in enumerate(
            ((kp, k_scr, 0), (ko, k_scr, 1), (kn, k_scr, 2),
             (vp, v_scr, 0), (vo, v_scr, 1), (vn, v_scr, 2))
        ):
            copy = pltpu.make_async_copy(
                src, dst.at[pl.ds(part * shard_rows, shard_rows)], sem.at[i]
            )
            copy.start()
            copies.append(copy)
        for copy in copies:
            copy.wait()

    scale = HD ** (-0.5)
    amount = cnt_ref[b]
    m_scr[...] = jnp.full(m_scr.shape, -jnp.inf, jnp.float32)
    for j in range(MAXB):
        @pl.when(j < amount)
        def _scores():
            start = pl.multiple_of(idx_ref[b * MAXB + j] * BLOCK, BLOCK)
            key_block = k_scr[pl.ds(start, BLOCK), :]
            scores = lax.dot_general(
                q_ref[...], key_block, (((1,), (1,)), ((), ())),
                preferred_element_type=jnp.float32,
            ) * scale
            s_scr[j] = scores
            m_scr[...] = jnp.maximum(m_scr[...], jnp.max(scores, axis=1, keepdims=True))

    l_scr[...] = jnp.zeros(l_scr.shape, jnp.float32)
    acc_scr[...] = jnp.zeros(acc_scr.shape, jnp.float32)
    for j in range(MAXB):
        @pl.when(j < amount)
        def _mix():
            start = pl.multiple_of(idx_ref[b * MAXB + j] * BLOCK, BLOCK)
            value_block = v_scr[pl.ds(start, BLOCK), :]
            expo = jnp.exp(s_scr[j] - m_scr[...])
            l_scr[...] += jnp.sum(expo, axis=1, keepdims=True)
            acc_scr[...] += jnp.dot(
                expo.astype(jnp.bfloat16), value_block, preferred_element_type=jnp.float32
            )

    o_ref[...] = (acc_scr[...] / l_scr[...]).astype(o_ref.dtype)


def attend(query_rows, k_parts, v_parts, local_index, count_rows):
    rows, width = query_rows.shape
    blocks_here = rows // BLOCK
    shard_rows = k_parts[0].shape[0]
    flops = blocks_here * MAXB * BLOCK * BLOCK * width * 4
    cost = pl.CostEstimate(
        flops=flops,
        transcendentals=blocks_here * MAXB * BLOCK * BLOCK,
        bytes_accessed=(2 + 6) * rows * width * 2,
    )
    any_spec = pl.BlockSpec(memory_space=pl.ANY)
    grid_spec = pltpu.PrefetchScalarGridSpec(
        num_scalar_prefetch=2,
        grid=(blocks_here,),
        in_specs=[pl.BlockSpec((BLOCK, width), lambda b, idx, cnt: (b, 0))] + [any_spec] * 6,
        out_specs=pl.BlockSpec((BLOCK, width), lambda b, idx, cnt: (b, 0)),
        scratch_shapes=[
            pltpu.VMEM((3 * shard_rows, width), jnp.bfloat16),
            pltpu.VMEM((3 * shard_rows, width), jnp.bfloat16),
            pltpu.VMEM((MAXB, BLOCK, BLOCK), jnp.float32),
            pltpu.VMEM((BLOCK, 1), jnp.float32),
            pltpu.VMEM((BLOCK, 1), jnp.float32),
            pltpu.VMEM((BLOCK, width), jnp.float32),
            pltpu.SemaphoreType.DMA((6,)),
        ],
    )
    return pl.pallas_call(
        functools.partial(attention_kernel, shard_rows=shard_rows),
        out_shape=jax.ShapeDtypeStruct((rows, width), jnp.bfloat16),
        grid_spec=grid_spec,
        compiler_params=pltpu.CompilerParams(dimension_semantics=("arbitrary",)),
        cost_estimate=cost,
    )(local_index, count_rows, query_rows, *k_parts, *v_parts)


def local(queries, keys, values, key_blocks, counts):
    cycle_size = lax.axis_size("blk")

    def to_heads(x):
        return lax.all_to_all(x, "head", split_axis=1, concat_axis=0, tiled=True)

    key_rows = to_heads(keys)
    value_rows = to_heads(values)
    query_rows = to_heads(queries)
    k_parts = (from_behind(key_rows, "blk", 1), key_rows, from_behind(key_rows, "blk", -1))
    v_parts = (from_behind(value_rows, "blk", 1), value_rows, from_behind(value_rows, "blk", -1))
    blocks_here = query_rows.shape[0] // BLOCK
    total_blocks = blocks_here * cycle_size
    first_block = lax.axis_index("blk") * blocks_here
    listed_rows = lax.dynamic_slice_in_dim(key_blocks, first_block, blocks_here, 0)
    count_rows = lax.dynamic_slice_in_dim(counts, first_block, blocks_here, 0)
    local_index = jnp.mod(listed_rows - first_block + blocks_here, total_blocks)
    local_index = jnp.clip(local_index, 0, 3 * blocks_here - 1).reshape(-1)
    attended_rows = attend(query_rows, k_parts, v_parts, local_index, count_rows)
    return lax.all_to_all(attended_rows, "head", split_axis=0, concat_axis=1, tiled=True)


def solution(mesh):
    placed = (
        P(("blk", "head"), None),
        P(("blk", "head"), None),
        P(("blk", "head"), None),
        P(),
        P(),
    )
    return jax.shard_map(
        local, mesh=mesh, in_specs=placed, out_specs=P(("blk", "head"), None), check_vma=False
    )
```

```python
import functools

import jax
import jax.numpy as jnp
from jax import lax
from jax.experimental import pallas as pl
from jax.experimental.pallas import tpu as pltpu
from jax.sharding import PartitionSpec as P

HD = 128
BLOCK = 512
MAXB = 6


def from_behind(value, axis, steps):
    count = lax.axis_size(axis)
    pairs = [(source, (source + steps) % count) for source in range(count)]
    return lax.ppermute(value, axis, pairs)


def attention_kernel(idx_ref, cnt_ref, q_ref, kv_prev, kv_own, kv_next, o_ref,
                     k_scr, v_scr, s_scr, m_scr, l_scr, acc_scr, sem, *, shard_rows):
    b = pl.program_id(0)
    width = q_ref.shape[1]

    @pl.when(b == 0)
    def _load_context():
        copies = []
        for i, (src, dst, part) in enumerate(
            ((kv_own.at[:, pl.ds(0, width)], k_scr, 1),
             (kv_own.at[:, pl.ds(width, width)], v_scr, 1),
             (kv_prev.at[:, pl.ds(0, width)], k_scr, 0),
             (kv_next.at[:, pl.ds(0, width)], k_scr, 2),
             (kv_prev.at[:, pl.ds(width, width)], v_scr, 0),
             (kv_next.at[:, pl.ds(width, width)], v_scr, 2))
        ):
            copy = pltpu.make_async_copy(
                src, dst.at[pl.ds(part * shard_rows, shard_rows)], sem.at[i]
            )
            copy.start()
            copies.append(copy)
        for copy in copies:
            copy.wait()

    scale = HD ** (-0.5)
    amount = cnt_ref[b]
    m_scr[...] = jnp.full(m_scr.shape, -jnp.inf, jnp.float32)
    for j in range(MAXB):
        @pl.when(j < amount)
        def _scores():
            start = pl.multiple_of(idx_ref[b * MAXB + j] * BLOCK, BLOCK)
            key_block = k_scr[pl.ds(start, BLOCK), :]
            scores = lax.dot_general(
                q_ref[...], key_block, (((1,), (1,)), ((), ())),
                preferred_element_type=jnp.float32,
            ) * scale
            s_scr[j] = scores
            m_scr[...] = jnp.maximum(m_scr[...], jnp.max(scores, axis=1, keepdims=True))

    l_scr[...] = jnp.zeros(l_scr.shape, jnp.float32)
    acc_scr[...] = jnp.zeros(acc_scr.shape, jnp.float32)
    for j in range(MAXB):
        @pl.when(j < amount)
        def _mix():
            start = pl.multiple_of(idx_ref[b * MAXB + j] * BLOCK, BLOCK)
            value_block = v_scr[pl.ds(start, BLOCK), :]
            expo = jnp.exp(s_scr[j] - m_scr[...])
            l_scr[...] += jnp.sum(expo, axis=1, keepdims=True)
            acc_scr[...] += jnp.dot(
                expo.astype(jnp.bfloat16), value_block, preferred_element_type=jnp.float32
            )

    o_ref[...] = (acc_scr[...] / l_scr[...]).astype(o_ref.dtype)


def attend(query_rows, kv_parts, local_index, count_rows):
    rows, width = query_rows.shape
    blocks_here = rows // BLOCK
    shard_rows = kv_parts[0].shape[0]
    flops = blocks_here * MAXB * BLOCK * BLOCK * width * 4
    cost = pl.CostEstimate(
        flops=flops,
        transcendentals=blocks_here * MAXB * BLOCK * BLOCK,
        bytes_accessed=(2 + 6) * rows * width * 2,
    )
    any_spec = pl.BlockSpec(memory_space=pl.ANY)
    grid_spec = pltpu.PrefetchScalarGridSpec(
        num_scalar_prefetch=2,
        grid=(blocks_here,),
        in_specs=[pl.BlockSpec((BLOCK, width), lambda b, idx, cnt: (b, 0))] + [any_spec] * 3,
        out_specs=pl.BlockSpec((BLOCK, width), lambda b, idx, cnt: (b, 0)),
        scratch_shapes=[
            pltpu.VMEM((3 * shard_rows, width), jnp.bfloat16),
            pltpu.VMEM((3 * shard_rows, width), jnp.bfloat16),
            pltpu.VMEM((MAXB, BLOCK, BLOCK), jnp.float32),
            pltpu.VMEM((BLOCK, 1), jnp.float32),
            pltpu.VMEM((BLOCK, 1), jnp.float32),
            pltpu.VMEM((BLOCK, width), jnp.float32),
            pltpu.SemaphoreType.DMA((6,)),
        ],
    )
    return pl.pallas_call(
        functools.partial(attention_kernel, shard_rows=shard_rows),
        out_shape=jax.ShapeDtypeStruct((rows, width), jnp.bfloat16),
        grid_spec=grid_spec,
        compiler_params=pltpu.CompilerParams(dimension_semantics=("arbitrary",)),
        cost_estimate=cost,
    )(local_index, count_rows, query_rows, *kv_parts)


def local(queries, keys, values, key_blocks, counts):
    cycle_size = lax.axis_size("blk")

    def to_heads(x):
        return lax.all_to_all(x, "head", split_axis=1, concat_axis=0, tiled=True)

    rows, model = keys.shape
    heads = model // HD
    paired = jnp.stack(
        [keys.reshape(rows, heads, HD), values.reshape(rows, heads, HD)], axis=2
    ).reshape(rows, 2 * model)
    kv_rows = to_heads(paired)
    query_rows = to_heads(queries)
    kv_parts = (from_behind(kv_rows, "blk", 1), kv_rows, from_behind(kv_rows, "blk", -1))
    blocks_here = query_rows.shape[0] // BLOCK
    total_blocks = blocks_here * cycle_size
    first_block = lax.axis_index("blk") * blocks_here
    listed_rows = lax.dynamic_slice_in_dim(key_blocks, first_block, blocks_here, 0)
    count_rows = lax.dynamic_slice_in_dim(counts, first_block, blocks_here, 0)
    local_index = jnp.mod(listed_rows - first_block + blocks_here, total_blocks)
    local_index = jnp.clip(local_index, 0, 3 * blocks_here - 1).reshape(-1)
    attended_rows = attend(query_rows, kv_parts, local_index, count_rows)
    return lax.all_to_all(attended_rows, "head", split_axis=0, concat_axis=1, tiled=True)


def solution(mesh):
    placed = (
        P(("blk", "head"), None),
        P(("blk", "head"), None),
        P(("blk", "head"), None),
        P(),
        P(),
    )
    return jax.shard_map(
        local, mesh=mesh, in_specs=placed, out_specs=P(("blk", "head"), None), check_vma=False
    )
```

```python
import functools

import jax
import jax.numpy as jnp
from jax import lax
from jax.experimental import pallas as pl
from jax.experimental.pallas import tpu as pltpu
from jax.sharding import PartitionSpec as P

HD = 128
BLOCK = 512
MAXB = 6


def from_behind(value, axis, steps):
    count = lax.axis_size(axis)
    pairs = [(source, (source + steps) % count) for source in range(count)]
    return lax.ppermute(value, axis, pairs)


def attention_kernel(idx_ref, cnt_ref, q_ref, kv_prev, kv_own, kv_next, o_ref,
                     k_scr, v_scr, s_scr, m_scr, l_scr, acc_scr, sem, *, shard_rows):
    b = pl.program_id(0)
    width = q_ref.shape[1]

    @pl.when(b == 0)
    def _load_context():
        copies = []
        for i, (src, dst, part) in enumerate(
            ((kv_own.at[:, pl.ds(0, width)], k_scr, 1),
             (kv_own.at[:, pl.ds(width, width)], v_scr, 1),
             (kv_prev.at[:, pl.ds(0, width)], k_scr, 0),
             (kv_next.at[:, pl.ds(0, width)], k_scr, 2),
             (kv_prev.at[:, pl.ds(width, width)], v_scr, 0),
             (kv_next.at[:, pl.ds(width, width)], v_scr, 2))
        ):
            copy = pltpu.make_async_copy(
                src, dst.at[pl.ds(part * shard_rows, shard_rows)], sem.at[i]
            )
            copy.start()
            copies.append(copy)
        for copy in copies:
            copy.wait()

    scale = HD ** (-0.5)
    amount = cnt_ref[b]
    m_scr[...] = jnp.full(m_scr.shape, -jnp.inf, jnp.float32)
    for j in range(MAXB):
        @pl.when(j < amount)
        def _scores():
            start = pl.multiple_of(idx_ref[b * MAXB + j] * BLOCK, BLOCK)
            key_block = k_scr[pl.ds(start, BLOCK), :]
            scores = lax.dot_general(
                q_ref[...], key_block, (((1,), (1,)), ((), ())),
                preferred_element_type=jnp.float32,
            ) * scale
            s_scr[j] = scores
            m_scr[...] = jnp.maximum(m_scr[...], jnp.max(scores, axis=1, keepdims=True))

    l_scr[...] = jnp.zeros(l_scr.shape, jnp.float32)
    acc_scr[...] = jnp.zeros(acc_scr.shape, jnp.float32)
    for j in range(MAXB):
        @pl.when(j < amount)
        def _mix():
            start = pl.multiple_of(idx_ref[b * MAXB + j] * BLOCK, BLOCK)
            value_block = v_scr[pl.ds(start, BLOCK), :]
            expo = jnp.exp(s_scr[j] - m_scr[...])
            l_scr[...] += jnp.sum(expo, axis=1, keepdims=True)
            acc_scr[...] += jnp.dot(
                expo.astype(jnp.bfloat16), value_block, preferred_element_type=jnp.float32
            )

    o_ref[...] = (acc_scr[...] / l_scr[...]).astype(o_ref.dtype)


def attend(query_rows, kv_parts, local_index, count_rows):
    rows, width = query_rows.shape
    shard_rows = kv_parts[0].shape[0]
    blocks_here = shard_rows // BLOCK
    q_block = rows // blocks_here
    flops = blocks_here * MAXB * q_block * BLOCK * width * 4
    cost = pl.CostEstimate(
        flops=flops,
        transcendentals=blocks_here * MAXB * q_block * BLOCK,
        bytes_accessed=(2 * rows + 6 * shard_rows) * width * 2,
    )
    any_spec = pl.BlockSpec(memory_space=pl.ANY)
    grid_spec = pltpu.PrefetchScalarGridSpec(
        num_scalar_prefetch=2,
        grid=(blocks_here,),
        in_specs=[pl.BlockSpec((q_block, width), lambda b, idx, cnt: (b, 0))] + [any_spec] * 3,
        out_specs=pl.BlockSpec((q_block, width), lambda b, idx, cnt: (b, 0)),
        scratch_shapes=[
            pltpu.VMEM((3 * shard_rows, width), jnp.bfloat16),
            pltpu.VMEM((3 * shard_rows, width), jnp.bfloat16),
            pltpu.VMEM((MAXB, q_block, BLOCK), jnp.float32),
            pltpu.VMEM((q_block, 1), jnp.float32),
            pltpu.VMEM((q_block, 1), jnp.float32),
            pltpu.VMEM((q_block, width), jnp.float32),
            pltpu.SemaphoreType.DMA((6,)),
        ],
    )
    return pl.pallas_call(
        functools.partial(attention_kernel, shard_rows=shard_rows),
        out_shape=jax.ShapeDtypeStruct((rows, width), jnp.bfloat16),
        grid_spec=grid_spec,
        compiler_params=pltpu.CompilerParams(dimension_semantics=("arbitrary",)),
        cost_estimate=cost,
    )(local_index, count_rows, query_rows, *kv_parts)


def local(queries, keys, values, key_blocks, counts):
    cycle_size = lax.axis_size("blk")

    def to_heads(x):
        return lax.all_to_all(x, "head", split_axis=1, concat_axis=0, tiled=True)

    rows, model = keys.shape
    heads = model // HD
    paired = jnp.stack(
        [keys.reshape(rows, heads, HD), values.reshape(rows, heads, HD)], axis=2
    ).reshape(rows, 2 * model)
    kv_rows = to_heads(paired)
    half = rows // 2
    query_halves = [to_heads(queries[:half]), to_heads(queries[half:])]
    kv_parts = (from_behind(kv_rows, "blk", 1), kv_rows, from_behind(kv_rows, "blk", -1))
    blocks_here = kv_rows.shape[0] // BLOCK
    total_blocks = blocks_here * cycle_size
    first_block = lax.axis_index("blk") * blocks_here
    listed_rows = lax.dynamic_slice_in_dim(key_blocks, first_block, blocks_here, 0)
    count_rows = lax.dynamic_slice_in_dim(counts, first_block, blocks_here, 0)
    local_index = jnp.mod(listed_rows - first_block + blocks_here, total_blocks)
    local_index = jnp.clip(local_index, 0, 3 * blocks_here - 1).reshape(-1)
    outs = []
    for query_rows in query_halves:
        attended_rows = attend(query_rows, kv_parts, local_index, count_rows)
        outs.append(lax.all_to_all(attended_rows, "head", split_axis=0, concat_axis=1, tiled=True))
    return jnp.concatenate(outs, axis=0)


def solution(mesh):
    placed = (
        P(("blk", "head"), None),
        P(("blk", "head"), None),
        P(("blk", "head"), None),
        P(),
        P(),
    )
    return jax.shard_map(
        local, mesh=mesh, in_specs=placed, out_specs=P(("blk", "head"), None), check_vma=False
    )
```

```python
import functools

import jax
import jax.numpy as jnp
from jax import lax
from jax.experimental import pallas as pl
from jax.experimental.pallas import tpu as pltpu
from jax.sharding import PartitionSpec as P

HD = 128
BLOCK = 512
MAXB = 6


def from_behind(value, axis, steps):
    count = lax.axis_size(axis)
    pairs = [(source, (source + steps) % count) for source in range(count)]
    return lax.ppermute(value, axis, pairs)


def attention_kernel(idx_ref, cnt_ref, q_ref, kv_prev, kv_own, kv_next, o_ref,
                     k_scr, v_scr, s_scr, m_scr, l_scr, acc_scr, sem, *, shard_rows):
    b = pl.program_id(0)
    width = q_ref.shape[1]

    @pl.when(b == 0)
    def _load_context():
        copies = []
        for i, (src, dst, part) in enumerate(
            ((kv_own.at[:, pl.ds(0, width)], k_scr, 1),
             (kv_own.at[:, pl.ds(width, width)], v_scr, 1),
             (kv_prev.at[:, pl.ds(0, width)], k_scr, 0),
             (kv_next.at[:, pl.ds(0, width)], k_scr, 2),
             (kv_prev.at[:, pl.ds(width, width)], v_scr, 0),
             (kv_next.at[:, pl.ds(width, width)], v_scr, 2))
        ):
            copy = pltpu.make_async_copy(
                src, dst.at[pl.ds(part * shard_rows, shard_rows)], sem.at[i]
            )
            copy.start()
            copies.append(copy)
        for copy in copies:
            copy.wait()

    scale = HD ** (-0.5)
    amount = cnt_ref[b]
    m_scr[...] = jnp.full(m_scr.shape, -jnp.inf, jnp.float32)
    for j in range(MAXB):
        @pl.when(j < amount)
        def _scores():
            start = pl.multiple_of(idx_ref[b * MAXB + j] * BLOCK, BLOCK)
            key_block = k_scr[pl.ds(start, BLOCK), :]
            scores = lax.dot_general(
                key_block, q_ref[...], (((1,), (1,)), ((), ())),
                preferred_element_type=jnp.float32,
            ) * scale
            s_scr[j] = scores
            m_scr[...] = jnp.maximum(m_scr[...], jnp.max(scores, axis=0, keepdims=True))

    l_scr[...] = jnp.zeros(l_scr.shape, jnp.float32)
    acc_scr[...] = jnp.zeros(acc_scr.shape, jnp.float32)
    for j in range(MAXB):
        @pl.when(j < amount)
        def _mix():
            start = pl.multiple_of(idx_ref[b * MAXB + j] * BLOCK, BLOCK)
            value_block = v_scr[pl.ds(start, BLOCK), :]
            expo = jnp.exp(s_scr[j] - m_scr[...])
            l_scr[...] += jnp.sum(expo, axis=0, keepdims=True)
            acc_scr[...] += lax.dot_general(
                value_block, expo.astype(jnp.bfloat16), (((0,), (0,)), ((), ())),
                preferred_element_type=jnp.float32,
            )

    o_ref[...] = jnp.transpose(acc_scr[...] / l_scr[...]).astype(o_ref.dtype)


def attend(query_rows, kv_parts, local_index, count_rows):
    rows, width = query_rows.shape
    blocks_here = rows // BLOCK
    shard_rows = kv_parts[0].shape[0]
    flops = blocks_here * MAXB * BLOCK * BLOCK * width * 4
    cost = pl.CostEstimate(
        flops=flops,
        transcendentals=blocks_here * MAXB * BLOCK * BLOCK,
        bytes_accessed=(2 + 6) * rows * width * 2,
    )
    any_spec = pl.BlockSpec(memory_space=pl.ANY)
    grid_spec = pltpu.PrefetchScalarGridSpec(
        num_scalar_prefetch=2,
        grid=(blocks_here,),
        in_specs=[pl.BlockSpec((BLOCK, width), lambda b, idx, cnt: (b, 0))] + [any_spec] * 3,
        out_specs=pl.BlockSpec((BLOCK, width), lambda b, idx, cnt: (b, 0)),
        scratch_shapes=[
            pltpu.VMEM((3 * shard_rows, width), jnp.bfloat16),
            pltpu.VMEM((3 * shard_rows, width), jnp.bfloat16),
            pltpu.VMEM((MAXB, BLOCK, BLOCK), jnp.float32),
            pltpu.VMEM((1, BLOCK), jnp.float32),
            pltpu.VMEM((1, BLOCK), jnp.float32),
            pltpu.VMEM((width, BLOCK), jnp.float32),
            pltpu.SemaphoreType.DMA((6,)),
        ],
    )
    return pl.pallas_call(
        functools.partial(attention_kernel, shard_rows=shard_rows),
        out_shape=jax.ShapeDtypeStruct((rows, width), jnp.bfloat16),
        grid_spec=grid_spec,
        compiler_params=pltpu.CompilerParams(dimension_semantics=("arbitrary",)),
        cost_estimate=cost,
    )(local_index, count_rows, query_rows, *kv_parts)


def local(queries, keys, values, key_blocks, counts):
    cycle_size = lax.axis_size("blk")

    def to_heads(x):
        return lax.all_to_all(x, "head", split_axis=1, concat_axis=0, tiled=True)

    rows, model = keys.shape
    heads = model // HD
    paired = jnp.stack(
        [keys.reshape(rows, heads, HD), values.reshape(rows, heads, HD)], axis=2
    ).reshape(rows, 2 * model)
    kv_rows = to_heads(paired)
    query_rows = to_heads(queries)
    kv_parts = (from_behind(kv_rows, "blk", 1), kv_rows, from_behind(kv_rows, "blk", -1))
    blocks_here = query_rows.shape[0] // BLOCK
    total_blocks = blocks_here * cycle_size
    first_block = lax.axis_index("blk") * blocks_here
    listed_rows = lax.dynamic_slice_in_dim(key_blocks, first_block, blocks_here, 0)
    count_rows = lax.dynamic_slice_in_dim(counts, first_block, blocks_here, 0)
    local_index = jnp.mod(listed_rows - first_block + blocks_here, total_blocks)
    local_index = jnp.clip(local_index, 0, 3 * blocks_here - 1).reshape(-1)
    attended_rows = attend(query_rows, kv_parts, local_index, count_rows)
    return lax.all_to_all(attended_rows, "head", split_axis=0, concat_axis=1, tiled=True)


def solution(mesh):
    placed = (
        P(("blk", "head"), None),
        P(("blk", "head"), None),
        P(("blk", "head"), None),
        P(),
        P(),
    )
    return jax.shard_map(
        local, mesh=mesh, in_specs=placed, out_specs=P(("blk", "head"), None), check_vma=False
    )
```

```python
import functools

import jax
import jax.numpy as jnp
from jax import lax
from jax.experimental import pallas as pl
from jax.experimental.pallas import tpu as pltpu
from jax.sharding import PartitionSpec as P

HD = 128
BLOCK = 512
MAXB = 6


def from_behind(value, axis, steps):
    count = lax.axis_size(axis)
    pairs = [(source, (source + steps) % count) for source in range(count)]
    return lax.ppermute(value, axis, pairs)


def own_kernel(idx_ref, cnt_ref, q_ref, kv_own, m_ref, l_ref, acc_ref,
               k_scr, v_scr, s_scr, sem, *, blocks):
    b = pl.program_id(0)
    width = q_ref.shape[1]
    shard_rows = blocks * BLOCK

    @pl.when(b == 0)
    def _load_context():
        copies = [
            pltpu.make_async_copy(kv_own.at[:, pl.ds(0, width)], k_scr, sem.at[0]),
            pltpu.make_async_copy(kv_own.at[:, pl.ds(width, width)], v_scr, sem.at[1]),
        ]
        for copy in copies:
            copy.start()
        for copy in copies:
            copy.wait()

    scale = HD ** (-0.5)
    amount = cnt_ref[b]

    def usable(j):
        g = idx_ref[b * MAXB + j]
        return (j < amount) & (g >= blocks) & (g < 2 * blocks)

    def row(j):
        return pl.multiple_of((idx_ref[b * MAXB + j] - blocks) * BLOCK, BLOCK)

    m_ref[...] = jnp.full(m_ref.shape, -jnp.inf, jnp.float32)
    for j in range(MAXB):
        @pl.when(usable(j))
        def _scores():
            scores = lax.dot_general(
                k_scr[pl.ds(row(j), BLOCK), :], q_ref[...], (((1,), (1,)), ((), ())),
                preferred_element_type=jnp.float32,
            ) * scale
            s_scr[j] = scores
            m_ref[...] = jnp.maximum(m_ref[...], jnp.max(scores, axis=0, keepdims=True))

    l_ref[...] = jnp.zeros(l_ref.shape, jnp.float32)
    acc_ref[...] = jnp.zeros(acc_ref.shape, jnp.float32)
    for j in range(MAXB):
        @pl.when(usable(j))
        def _mix():
            expo = jnp.exp(s_scr[j] - m_ref[...])
            l_ref[...] += jnp.sum(expo, axis=0, keepdims=True)
            acc_ref[...] += lax.dot_general(
                v_scr[pl.ds(row(j), BLOCK), :], expo.astype(jnp.bfloat16),
                (((0,), (0,)), ((), ())), preferred_element_type=jnp.float32,
            )


def rest_kernel(idx_ref, cnt_ref, q_ref, m_in, l_in, acc_in, kv_prev, kv_next, o_ref,
                k_scr, v_scr, s_scr, m_scr, l_scr, acc_scr, sem, *, blocks):
    b = pl.program_id(0)
    width = q_ref.shape[1]
    shard_rows = blocks * BLOCK

    @pl.when(b == 0)
    def _load_context():
        copies = []
        for i, (src, dst, part) in enumerate(
            ((kv_prev.at[:, pl.ds(0, width)], k_scr, 0),
             (kv_next.at[:, pl.ds(0, width)], k_scr, 1),
             (kv_prev.at[:, pl.ds(width, width)], v_scr, 0),
             (kv_next.at[:, pl.ds(width, width)], v_scr, 1))
        ):
            copy = pltpu.make_async_copy(
                src, dst.at[pl.ds(part * shard_rows, shard_rows)], sem.at[i]
            )
            copy.start()
            copies.append(copy)
        for copy in copies:
            copy.wait()

    scale = HD ** (-0.5)
    amount = cnt_ref[b]

    def usable(j):
        g = idx_ref[b * MAXB + j]
        return (j < amount) & ((g < blocks) | (g >= 2 * blocks))

    def row(j):
        g = idx_ref[b * MAXB + j]
        return pl.multiple_of(jnp.where(g < blocks, g, g - blocks) * BLOCK, BLOCK)

    m_scr[...] = m_in[...]
    for j in range(MAXB):
        @pl.when(usable(j))
        def _scores():
            scores = lax.dot_general(
                k_scr[pl.ds(row(j), BLOCK), :], q_ref[...], (((1,), (1,)), ((), ())),
                preferred_element_type=jnp.float32,
            ) * scale
            s_scr[j] = scores
            m_scr[...] = jnp.maximum(m_scr[...], jnp.max(scores, axis=0, keepdims=True))

    alpha = jnp.exp(m_in[...] - m_scr[...])
    l_scr[...] = alpha * l_in[...]
    acc_scr[...] = alpha * acc_in[...]
    for j in range(MAXB):
        @pl.when(usable(j))
        def _mix():
            expo = jnp.exp(s_scr[j] - m_scr[...])
            l_scr[...] += jnp.sum(expo, axis=0, keepdims=True)
            acc_scr[...] += lax.dot_general(
                v_scr[pl.ds(row(j), BLOCK), :], expo.astype(jnp.bfloat16),
                (((0,), (0,)), ((), ())), preferred_element_type=jnp.float32,
            )

    o_ref[...] = jnp.transpose(acc_scr[...] / l_scr[...]).astype(o_ref.dtype)


def attend_own(query_rows, kv_own, local_index, count_rows):
    rows, width = query_rows.shape
    blocks = rows // BLOCK
    cost = pl.CostEstimate(
        flops=blocks * 4 * BLOCK * BLOCK * width * 4,
        transcendentals=blocks * 4 * BLOCK * BLOCK,
        bytes_accessed=rows * width * 2 * 3 + blocks * (width + 2) * BLOCK * 4,
    )
    q_spec = pl.BlockSpec((BLOCK, width), lambda b, idx, cnt: (b, 0))
    row_spec = pl.BlockSpec((None, 1, BLOCK), lambda b, idx, cnt: (b, 0, 0))
    acc_spec = pl.BlockSpec((None, width, BLOCK), lambda b, idx, cnt: (b, 0, 0))
    grid_spec = pltpu.PrefetchScalarGridSpec(
        num_scalar_prefetch=2,
        grid=(blocks,),
        in_specs=[q_spec, pl.BlockSpec(memory_space=pl.ANY)],
        out_specs=[row_spec, row_spec, acc_spec],
        scratch_shapes=[
            pltpu.VMEM((rows, width), jnp.bfloat16),
            pltpu.VMEM((rows, width), jnp.bfloat16),
            pltpu.VMEM((MAXB, BLOCK, BLOCK), jnp.float32),
            pltpu.SemaphoreType.DMA((2,)),
        ],
    )
    return pl.pallas_call(
        functools.partial(own_kernel, blocks=blocks),
        out_shape=[
            jax.ShapeDtypeStruct((blocks, 1, BLOCK), jnp.float32),
            jax.ShapeDtypeStruct((blocks, 1, BLOCK), jnp.float32),
            jax.ShapeDtypeStruct((blocks, width, BLOCK), jnp.float32),
        ],
        grid_spec=grid_spec,
        compiler_params=pltpu.CompilerParams(dimension_semantics=("arbitrary",)),
        cost_estimate=cost,
    )(local_index, count_rows, query_rows, kv_own)


def attend_rest(query_rows, partial, kv_prev, kv_next, local_index, count_rows):
    rows, width = query_rows.shape
    blocks = rows // BLOCK
    cost = pl.CostEstimate(
        flops=blocks * 2 * BLOCK * BLOCK * width * 4,
        transcendentals=blocks * 2 * BLOCK * BLOCK,
        bytes_accessed=rows * width * 2 * 6 + blocks * (width + 2) * BLOCK * 4,
    )
    q_spec = pl.BlockSpec((BLOCK, width), lambda b, idx, cnt: (b, 0))
    row_spec = pl.BlockSpec((None, 1, BLOCK), lambda b, idx, cnt: (b, 0, 0))
    acc_spec = pl.BlockSpec((None, width, BLOCK), lambda b, idx, cnt: (b, 0, 0))
    any_spec = pl.BlockSpec(memory_space=pl.ANY)
    grid_spec = pltpu.PrefetchScalarGridSpec(
        num_scalar_prefetch=2,
        grid=(blocks,),
        in_specs=[q_spec, row_spec, row_spec, acc_spec, any_spec, any_spec],
        out_specs=q_spec,
        scratch_shapes=[
            pltpu.VMEM((2 * rows, width), jnp.bfloat16),
            pltpu.VMEM((2 * rows, width), jnp.bfloat16),
            pltpu.VMEM((MAXB, BLOCK, BLOCK), jnp.float32),
            pltpu.VMEM((1, BLOCK), jnp.float32),
            pltpu.VMEM((1, BLOCK), jnp.float32),
            pltpu.VMEM((width, BLOCK), jnp.float32),
            pltpu.SemaphoreType.DMA((4,)),
        ],
    )
    return pl.pallas_call(
        functools.partial(rest_kernel, blocks=blocks),
        out_shape=jax.ShapeDtypeStruct((rows, width), jnp.bfloat16),
        grid_spec=grid_spec,
        compiler_params=pltpu.CompilerParams(dimension_semantics=("arbitrary",)),
        cost_estimate=cost,
    )(local_index, count_rows, query_rows, *partial, kv_prev, kv_next)


def local(queries, keys, values, key_blocks, counts):
    cycle_size = lax.axis_size("blk")

    def to_heads(x):
        return lax.all_to_all(x, "head", split_axis=1, concat_axis=0, tiled=True)

    rows, model = keys.shape
    heads = model // HD
    query_rows = to_heads(queries)
    after_queries = (query_rows[0, 0] * 0).astype(keys.dtype)
    paired = jnp.stack(
        [keys.reshape(rows, heads, HD), values.reshape(rows, heads, HD) + after_queries], axis=2
    ).reshape(rows, 2 * model)
    kv_rows = to_heads(paired)
    blocks_here = query_rows.shape[0] // BLOCK
    total_blocks = blocks_here * cycle_size
    first_block = lax.axis_index("blk") * blocks_here
    listed_rows = lax.dynamic_slice_in_dim(key_blocks, first_block, blocks_here, 0)
    count_rows = lax.dynamic_slice_in_dim(counts, first_block, blocks_here, 0)
    local_index = jnp.mod(listed_rows - first_block + blocks_here, total_blocks)
    local_index = jnp.clip(local_index, 0, 3 * blocks_here - 1).reshape(-1)
    partial = attend_own(query_rows, kv_rows, local_index, count_rows)
    kv_prev = from_behind(kv_rows, "blk", 1)
    kv_next = from_behind(kv_rows, "blk", -1)
    attended_rows = attend_rest(query_rows, partial, kv_prev, kv_next, local_index, count_rows)
    return lax.all_to_all(attended_rows, "head", split_axis=0, concat_axis=1, tiled=True)


def solution(mesh):
    placed = (
        P(("blk", "head"), None),
        P(("blk", "head"), None),
        P(("blk", "head"), None),
        P(),
        P(),
    )
    return jax.shard_map(
        local, mesh=mesh, in_specs=placed, out_specs=P(("blk", "head"), None), check_vma=False
    )
```

```python
import functools

import jax
import jax.numpy as jnp
from jax import lax
from jax.experimental import pallas as pl
from jax.experimental.pallas import tpu as pltpu
from jax.sharding import PartitionSpec as P

HD = 128
BLOCK = 512
MAXB = 6
TILES = 4


def from_behind(value, axis, steps):
    count = lax.axis_size(axis)
    pairs = [(source, (source + steps) % count) for source in range(count)]
    return lax.ppermute(value, axis, pairs)


def attention_kernel(idx_ref, cnt_ref, q_ref, kv_prev, kv_own, kv_next, o_ref,
                     k_scr, v_scr, s_scr, m_scr, l_scr, acc_scr, sem):
    b = pl.program_id(0)
    sources = kv_own.shape[0]

    @pl.when(b == 0)
    def _load_context():
        copies = []
        for i, (src, dst, part) in enumerate(
            ((kv_own.at[:, 0], k_scr, 1),
             (kv_own.at[:, 1], v_scr, 1),
             (kv_prev.at[:, 0], k_scr, 0),
             (kv_next.at[:, 0], k_scr, 2),
             (kv_prev.at[:, 1], v_scr, 0),
             (kv_next.at[:, 1], v_scr, 2))
        ):
            copy = pltpu.make_async_copy(
                src, dst.at[pl.ds(part * sources, sources)], sem.at[i]
            )
            copy.start()
            copies.append(copy)
        for copy in copies:
            copy.wait()

    scale = HD ** (-0.5)
    amount = cnt_ref[b]
    m_scr[...] = jnp.full(m_scr.shape, -jnp.inf, jnp.float32)
    for j in range(MAXB):
        @pl.when(j < amount)
        def _scores():
            start = pl.multiple_of(idx_ref[b * MAXB + j] * TILES, TILES)
            key_block = k_scr[pl.ds(start, TILES)].reshape(BLOCK, HD)
            scores = lax.dot_general(
                key_block, q_ref[...], (((1,), (1,)), ((), ())),
                preferred_element_type=jnp.float32,
            ) * scale
            s_scr[j] = scores
            m_scr[...] = jnp.maximum(m_scr[...], jnp.max(scores, axis=0, keepdims=True))

    l_scr[...] = jnp.zeros(l_scr.shape, jnp.float32)
    acc_scr[...] = jnp.zeros(acc_scr.shape, jnp.float32)
    for j in range(MAXB):
        @pl.when(j < amount)
        def _mix():
            start = pl.multiple_of(idx_ref[b * MAXB + j] * TILES, TILES)
            value_block = v_scr[pl.ds(start, TILES)].reshape(BLOCK, HD)
            expo = jnp.exp(s_scr[j] - m_scr[...])
            l_scr[...] += jnp.sum(expo, axis=0, keepdims=True)
            acc_scr[...] += lax.dot_general(
                value_block, expo.astype(jnp.bfloat16), (((0,), (0,)), ((), ())),
                preferred_element_type=jnp.float32,
            )

    o_ref[...] = jnp.transpose(acc_scr[...] / l_scr[...]).astype(o_ref.dtype)


def attend(query_rows, kv_parts, local_index, count_rows):
    rows, width = query_rows.shape
    blocks_here = rows // BLOCK
    sources, _, tile, _ = kv_parts[0].shape
    flops = blocks_here * MAXB * BLOCK * BLOCK * width * 4
    cost = pl.CostEstimate(
        flops=flops,
        transcendentals=blocks_here * MAXB * BLOCK * BLOCK,
        bytes_accessed=(2 + 6) * rows * width * 2,
    )
    any_spec = pl.BlockSpec(memory_space=pl.ANY)
    grid_spec = pltpu.PrefetchScalarGridSpec(
        num_scalar_prefetch=2,
        grid=(blocks_here,),
        in_specs=[pl.BlockSpec((BLOCK, width), lambda b, idx, cnt: (b, 0))] + [any_spec] * 3,
        out_specs=pl.BlockSpec((BLOCK, width), lambda b, idx, cnt: (b, 0)),
        scratch_shapes=[
            pltpu.VMEM((3 * sources, tile, width), jnp.bfloat16),
            pltpu.VMEM((3 * sources, tile, width), jnp.bfloat16),
            pltpu.VMEM((MAXB, BLOCK, BLOCK), jnp.float32),
            pltpu.VMEM((1, BLOCK), jnp.float32),
            pltpu.VMEM((1, BLOCK), jnp.float32),
            pltpu.VMEM((width, BLOCK), jnp.float32),
            pltpu.SemaphoreType.DMA((6,)),
        ],
    )
    return pl.pallas_call(
        attention_kernel,
        out_shape=jax.ShapeDtypeStruct((rows, width), jnp.bfloat16),
        grid_spec=grid_spec,
        compiler_params=pltpu.CompilerParams(dimension_semantics=("arbitrary",)),
        cost_estimate=cost,
    )(local_index, count_rows, query_rows, *kv_parts)


def local(queries, keys, values, key_blocks, counts):
    cycle_size = lax.axis_size("blk")

    def to_heads(x):
        return lax.all_to_all(x, "head", split_axis=1, concat_axis=0, tiled=True)

    rows = keys.shape[0]
    kv_rows = to_heads(jnp.concatenate([keys, values], axis=0))
    kv_rows = kv_rows.reshape(lax.axis_size("head"), 2, rows, HD)
    query_rows = to_heads(queries)
    kv_parts = (from_behind(kv_rows, "blk", 1), kv_rows, from_behind(kv_rows, "blk", -1))
    blocks_here = query_rows.shape[0] // BLOCK
    total_blocks = blocks_here * cycle_size
    first_block = lax.axis_index("blk") * blocks_here
    listed_rows = lax.dynamic_slice_in_dim(key_blocks, first_block, blocks_here, 0)
    count_rows = lax.dynamic_slice_in_dim(counts, first_block, blocks_here, 0)
    local_index = jnp.mod(listed_rows - first_block + blocks_here, total_blocks)
    local_index = jnp.clip(local_index, 0, 3 * blocks_here - 1).reshape(-1)
    attended_rows = attend(query_rows, kv_parts, local_index, count_rows)
    return lax.all_to_all(attended_rows, "head", split_axis=0, concat_axis=1, tiled=True)


def solution(mesh):
    placed = (
        P(("blk", "head"), None),
        P(("blk", "head"), None),
        P(("blk", "head"), None),
        P(),
        P(),
    )
    return jax.shard_map(
        local, mesh=mesh, in_specs=placed, out_specs=P(("blk", "head"), None), check_vma=False
    )
```

```python
import functools

import jax
import jax.numpy as jnp
from jax import lax
from jax.experimental import pallas as pl
from jax.experimental.pallas import tpu as pltpu
from jax.sharding import PartitionSpec as P

HD = 128
BLOCK = 512
MAXB = 6


def from_behind(value, axis, steps):
    count = lax.axis_size(axis)
    pairs = [(source, (source + steps) % count) for source in range(count)]
    return lax.ppermute(value, axis, pairs)


def attention_kernel(idx_ref, cnt_ref, q_ref, *refs):
    slabs, (o_ref, k_scr, v_scr, s_scr, m_scr, l_scr, acc_scr, sem) = refs[:6], refs[6:]
    b = pl.program_id(0)
    width = q_ref.shape[1]
    blocks = k_scr.shape[0] // 3

    @pl.when(b == 0)
    def _load_context():
        copies = []
        for i, slab in enumerate(slabs):
            part, half = (1, 0, 2)[i // 2], i % 2
            for column, dst in ((0, k_scr), (width, v_scr)):
                copy = pltpu.make_async_copy(
                    slab.at[:, :, pl.ds(column, width)],
                    dst.at[pl.ds(part * blocks, blocks), half],
                    sem.at[2 * i + column // width],
                )
                copy.start()
                copies.append(copy)
        for copy in copies:
            copy.wait()

    scale = HD ** (-0.5)
    amount = cnt_ref[b]
    m_scr[...] = jnp.full(m_scr.shape, -jnp.inf, jnp.float32)
    for j in range(MAXB):
        @pl.when(j < amount)
        def _scores():
            key_block = k_scr[idx_ref[b * MAXB + j]].reshape(BLOCK, HD)
            scores = lax.dot_general(
                key_block, q_ref[...], (((1,), (1,)), ((), ())),
                preferred_element_type=jnp.float32,
            ) * scale
            s_scr[j] = scores
            m_scr[...] = jnp.maximum(m_scr[...], jnp.max(scores, axis=0, keepdims=True))

    l_scr[...] = jnp.zeros(l_scr.shape, jnp.float32)
    acc_scr[...] = jnp.zeros(acc_scr.shape, jnp.float32)
    for j in range(MAXB):
        @pl.when(j < amount)
        def _mix():
            value_block = v_scr[idx_ref[b * MAXB + j]].reshape(BLOCK, HD)
            expo = jnp.exp(s_scr[j] - m_scr[...])
            l_scr[...] += jnp.sum(expo, axis=0, keepdims=True)
            acc_scr[...] += lax.dot_general(
                value_block, expo.astype(jnp.bfloat16), (((0,), (0,)), ((), ())),
                preferred_element_type=jnp.float32,
            )

    o_ref[...] = jnp.transpose(acc_scr[...] / l_scr[...]).astype(o_ref.dtype)


def attend(query_rows, kv_parts, local_index, count_rows):
    rows, width = query_rows.shape
    blocks_here = rows // BLOCK
    shard_rows = rows
    flops = blocks_here * MAXB * BLOCK * BLOCK * width * 4
    cost = pl.CostEstimate(
        flops=flops,
        transcendentals=blocks_here * MAXB * BLOCK * BLOCK,
        bytes_accessed=(2 + 6) * rows * width * 2,
    )
    any_spec = pl.BlockSpec(memory_space=pl.ANY)
    grid_spec = pltpu.PrefetchScalarGridSpec(
        num_scalar_prefetch=2,
        grid=(blocks_here,),
        in_specs=[pl.BlockSpec((BLOCK, width), lambda b, idx, cnt: (b, 0))] + [any_spec] * 6,
        out_specs=pl.BlockSpec((BLOCK, width), lambda b, idx, cnt: (b, 0)),
        scratch_shapes=[
            pltpu.VMEM((3 * blocks_here, 2, BLOCK // 2, width), jnp.bfloat16),
            pltpu.VMEM((3 * blocks_here, 2, BLOCK // 2, width), jnp.bfloat16),
            pltpu.VMEM((MAXB, BLOCK, BLOCK), jnp.float32),
            pltpu.VMEM((1, BLOCK), jnp.float32),
            pltpu.VMEM((1, BLOCK), jnp.float32),
            pltpu.VMEM((width, BLOCK), jnp.float32),
            pltpu.SemaphoreType.DMA((12,)),
        ],
    )
    return pl.pallas_call(
        attention_kernel,
        out_shape=jax.ShapeDtypeStruct((rows, width), jnp.bfloat16),
        grid_spec=grid_spec,
        compiler_params=pltpu.CompilerParams(dimension_semantics=("arbitrary",)),
        cost_estimate=cost,
    )(local_index, count_rows, query_rows, *kv_parts)


def local(queries, keys, values, key_blocks, counts):
    cycle_size = lax.axis_size("blk")

    def to_heads(x):
        return lax.all_to_all(x, "head", split_axis=1, concat_axis=0, tiled=True)

    rows, model = keys.shape
    heads = model // HD
    paired = jnp.stack(
        [keys.reshape(rows, heads, HD), values.reshape(rows, heads, HD)], axis=2
    ).reshape(rows, 2 * model)
    half = rows // 2
    kv_parts = []
    tie = None
    for piece in (paired[:half], paired[half:]):
        kv_rows = to_heads(piece)
        if tie is not None:
            kv_rows = kv_rows + tie
        earlier, later = from_behind(kv_rows, "blk", 1), from_behind(kv_rows, "blk", -1)
        tie = ((earlier[0, 0] + later[0, 0]) * 0).astype(kv_rows.dtype)
        kv_parts.append((kv_rows, earlier, later))
    query_rows = to_heads(queries)
    slab_shape = (lax.axis_size("head") * half // (BLOCK // 2), BLOCK // 2, 2 * HD)
    kv_parts = [kv_parts[h][p].reshape(slab_shape) for p in range(3) for h in range(2)]
    blocks_here = query_rows.shape[0] // BLOCK
    total_blocks = blocks_here * cycle_size
    first_block = lax.axis_index("blk") * blocks_here
    listed_rows = lax.dynamic_slice_in_dim(key_blocks, first_block, blocks_here, 0)
    count_rows = lax.dynamic_slice_in_dim(counts, first_block, blocks_here, 0)
    local_index = jnp.mod(listed_rows - first_block + blocks_here, total_blocks)
    local_index = jnp.clip(local_index, 0, 3 * blocks_here - 1).reshape(-1)
    attended_rows = attend(query_rows, kv_parts, local_index, count_rows)
    return lax.all_to_all(attended_rows, "head", split_axis=0, concat_axis=1, tiled=True)


def solution(mesh):
    placed = (
        P(("blk", "head"), None),
        P(("blk", "head"), None),
        P(("blk", "head"), None),
        P(),
        P(),
    )
    return jax.shard_map(
        local, mesh=mesh, in_specs=placed, out_specs=P(("blk", "head"), None), check_vma=False
    )
```

```python
import functools

import jax
import jax.numpy as jnp
from jax import lax
from jax.experimental import pallas as pl
from jax.experimental.pallas import tpu as pltpu
from jax.sharding import PartitionSpec as P

HD = 128
BLOCK = 512
MAXB = 6


def from_behind(value, axis, steps):
    count = lax.axis_size(axis)
    pairs = [(source, (source + steps) % count) for source in range(count)]
    return lax.ppermute(value, axis, pairs)


def load_slabs(slabs, k_scr, v_scr, sem, width, blocks):
    copies = []
    for i, slab in enumerate(slabs):
        part, half = i // 2, i % 2
        for column, dst in ((0, k_scr), (width, v_scr)):
            copy = pltpu.make_async_copy(
                slab.at[:, :, pl.ds(column, width)],
                dst.at[pl.ds(part * blocks, blocks), half],
                sem.at[2 * i + column // width],
            )
            copy.start()
            copies.append(copy)
    for copy in copies:
        copy.wait()


def own_kernel(idx_ref, cnt_ref, q_ref, own0, own1, m_ref, l_ref, acc_ref,
               k_scr, v_scr, s_scr, sem, *, blocks):
    b = pl.program_id(0)
    width = q_ref.shape[1]

    @pl.when(b == 0)
    def _load_context():
        load_slabs((own0, own1), k_scr, v_scr, sem, width, blocks)

    scale = HD ** (-0.5)
    amount = cnt_ref[b]

    def usable(j):
        g = idx_ref[b * MAXB + j]
        return (j < amount) & (g >= blocks) & (g < 2 * blocks)

    def row(j):
        return idx_ref[b * MAXB + j] - blocks

    m_ref[...] = jnp.full(m_ref.shape, -jnp.inf, jnp.float32)
    for j in range(MAXB):
        @pl.when(usable(j))
        def _scores():
            scores = lax.dot_general(
                k_scr[row(j)].reshape(BLOCK, HD), q_ref[...], (((1,), (1,)), ((), ())),
                preferred_element_type=jnp.float32,
            ) * scale
            s_scr[j] = scores
            m_ref[...] = jnp.maximum(m_ref[...], jnp.max(scores, axis=0, keepdims=True))

    l_ref[...] = jnp.zeros(l_ref.shape, jnp.float32)
    acc_ref[...] = jnp.zeros(acc_ref.shape, jnp.float32)
    for j in range(MAXB):
        @pl.when(usable(j))
        def _mix():
            expo = jnp.exp(s_scr[j] - m_ref[...])
            l_ref[...] += jnp.sum(expo, axis=0, keepdims=True)
            acc_ref[...] += lax.dot_general(
                v_scr[row(j)].reshape(BLOCK, HD), expo.astype(jnp.bfloat16),
                (((0,), (0,)), ((), ())), preferred_element_type=jnp.float32,
            )


def rest_kernel(idx_ref, cnt_ref, q_ref, m_in, l_in, acc_in, prev0, prev1, next0, next1,
                o_ref, k_scr, v_scr, s_scr, m_scr, l_scr, acc_scr, sem, *, blocks):
    b = pl.program_id(0)
    width = q_ref.shape[1]

    @pl.when(b == 0)
    def _load_context():
        load_slabs((prev0, prev1, next0, next1), k_scr, v_scr, sem, width, blocks)

    scale = HD ** (-0.5)
    amount = cnt_ref[b]

    def usable(j):
        g = idx_ref[b * MAXB + j]
        return (j < amount) & ((g < blocks) | (g >= 2 * blocks))

    def row(j):
        g = idx_ref[b * MAXB + j]
        return jnp.where(g < blocks, g, g - blocks)

    m_scr[...] = m_in[...]
    for j in range(MAXB):
        @pl.when(usable(j))
        def _scores():
            scores = lax.dot_general(
                k_scr[row(j)].reshape(BLOCK, HD), q_ref[...], (((1,), (1,)), ((), ())),
                preferred_element_type=jnp.float32,
            ) * scale
            s_scr[j] = scores
            m_scr[...] = jnp.maximum(m_scr[...], jnp.max(scores, axis=0, keepdims=True))

    alpha = jnp.exp(m_in[...] - m_scr[...])
    l_scr[...] = alpha * l_in[...]
    acc_scr[...] = alpha * acc_in[...]
    for j in range(MAXB):
        @pl.when(usable(j))
        def _mix():
            expo = jnp.exp(s_scr[j] - m_scr[...])
            l_scr[...] += jnp.sum(expo, axis=0, keepdims=True)
            acc_scr[...] += lax.dot_general(
                v_scr[row(j)].reshape(BLOCK, HD), expo.astype(jnp.bfloat16),
                (((0,), (0,)), ((), ())), preferred_element_type=jnp.float32,
            )

    o_ref[...] = jnp.transpose(acc_scr[...] / l_scr[...]).astype(o_ref.dtype)


def attend_own(query_rows, own_slabs, local_index, count_rows):
    rows, width = query_rows.shape
    blocks = rows // BLOCK
    cost = pl.CostEstimate(
        flops=blocks * 4 * BLOCK * BLOCK * width * 4,
        transcendentals=blocks * 4 * BLOCK * BLOCK,
        bytes_accessed=rows * width * 2 * 3 + blocks * (width + 2) * BLOCK * 4,
    )
    q_spec = pl.BlockSpec((BLOCK, width), lambda b, idx, cnt: (b, 0))
    row_spec = pl.BlockSpec((None, 1, BLOCK), lambda b, idx, cnt: (b, 0, 0))
    acc_spec = pl.BlockSpec((None, width, BLOCK), lambda b, idx, cnt: (b, 0, 0))
    grid_spec = pltpu.PrefetchScalarGridSpec(
        num_scalar_prefetch=2,
        grid=(blocks,),
        in_specs=[q_spec] + [pl.BlockSpec(memory_space=pl.ANY)] * 2,
        out_specs=[row_spec, row_spec, acc_spec],
        scratch_shapes=[
            pltpu.VMEM((blocks, 2, BLOCK // 2, width), jnp.bfloat16),
            pltpu.VMEM((blocks, 2, BLOCK // 2, width), jnp.bfloat16),
            pltpu.VMEM((MAXB, BLOCK, BLOCK), jnp.float32),
            pltpu.SemaphoreType.DMA((4,)),
        ],
    )
    return pl.pallas_call(
        functools.partial(own_kernel, blocks=blocks),
        out_shape=[
            jax.ShapeDtypeStruct((blocks, 1, BLOCK), jnp.float32),
            jax.ShapeDtypeStruct((blocks, 1, BLOCK), jnp.float32),
            jax.ShapeDtypeStruct((blocks, width, BLOCK), jnp.float32),
        ],
        grid_spec=grid_spec,
        compiler_params=pltpu.CompilerParams(dimension_semantics=("arbitrary",)),
        cost_estimate=cost,
    )(local_index, count_rows, query_rows, *own_slabs)


def attend_rest(query_rows, partial, side_slabs, local_index, count_rows):
    rows, width = query_rows.shape
    blocks = rows // BLOCK
    cost = pl.CostEstimate(
        flops=blocks * 2 * BLOCK * BLOCK * width * 4,
        transcendentals=blocks * 2 * BLOCK * BLOCK,
        bytes_accessed=rows * width * 2 * 6 + blocks * (width + 2) * BLOCK * 4,
    )
    q_spec = pl.BlockSpec((BLOCK, width), lambda b, idx, cnt: (b, 0))
    row_spec = pl.BlockSpec((None, 1, BLOCK), lambda b, idx, cnt: (b, 0, 0))
    acc_spec = pl.BlockSpec((None, width, BLOCK), lambda b, idx, cnt: (b, 0, 0))
    any_spec = pl.BlockSpec(memory_space=pl.ANY)
    grid_spec = pltpu.PrefetchScalarGridSpec(
        num_scalar_prefetch=2,
        grid=(blocks,),
        in_specs=[q_spec, row_spec, row_spec, acc_spec] + [any_spec] * 4,
        out_specs=q_spec,
        scratch_shapes=[
            pltpu.VMEM((2 * blocks, 2, BLOCK // 2, width), jnp.bfloat16),
            pltpu.VMEM((2 * blocks, 2, BLOCK // 2, width), jnp.bfloat16),
            pltpu.VMEM((MAXB, BLOCK, BLOCK), jnp.float32),
            pltpu.VMEM((1, BLOCK), jnp.float32),
            pltpu.VMEM((1, BLOCK), jnp.float32),
            pltpu.VMEM((width, BLOCK), jnp.float32),
            pltpu.SemaphoreType.DMA((8,)),
        ],
    )
    return pl.pallas_call(
        functools.partial(rest_kernel, blocks=blocks),
        out_shape=jax.ShapeDtypeStruct((rows, width), jnp.bfloat16),
        grid_spec=grid_spec,
        compiler_params=pltpu.CompilerParams(dimension_semantics=("arbitrary",)),
        cost_estimate=cost,
    )(local_index, count_rows, query_rows, *partial, *side_slabs)


def local(queries, keys, values, key_blocks, counts):
    cycle_size = lax.axis_size("blk")

    def to_heads(x):
        return lax.all_to_all(x, "head", split_axis=1, concat_axis=0, tiled=True)

    rows, model = keys.shape
    heads = model // HD
    paired = jnp.stack(
        [keys.reshape(rows, heads, HD), values.reshape(rows, heads, HD)], axis=2
    ).reshape(rows, 2 * model)
    half = rows // 2
    kv_parts = []
    tie = None
    for piece in (paired[:half], paired[half:]):
        kv_rows = to_heads(piece)
        if tie is not None:
            kv_rows = kv_rows + tie
        earlier, later = from_behind(kv_rows, "blk", 1), from_behind(kv_rows, "blk", -1)
        tie = ((earlier[0, 0] + later[0, 0]) * 0).astype(kv_rows.dtype)
        kv_parts.append((kv_rows, earlier, later))
    query_rows = to_heads(queries)
    slab_shape = (lax.axis_size("head") * half // (BLOCK // 2), BLOCK // 2, 2 * HD)
    kv_parts = [kv_parts[h][p].reshape(slab_shape) for p in range(3) for h in range(2)]
    own_slabs, side_slabs = kv_parts[:2], kv_parts[2:]
    blocks_here = query_rows.shape[0] // BLOCK
    total_blocks = blocks_here * cycle_size
    first_block = lax.axis_index("blk") * blocks_here
    listed_rows = lax.dynamic_slice_in_dim(key_blocks, first_block, blocks_here, 0)
    count_rows = lax.dynamic_slice_in_dim(counts, first_block, blocks_here, 0)
    local_index = jnp.mod(listed_rows - first_block + blocks_here, total_blocks)
    local_index = jnp.clip(local_index, 0, 3 * blocks_here - 1).reshape(-1)
    partial = attend_own(query_rows, own_slabs, local_index, count_rows)
    attended_rows = attend_rest(query_rows, partial, side_slabs, local_index, count_rows)
    return lax.all_to_all(attended_rows, "head", split_axis=0, concat_axis=1, tiled=True)


def solution(mesh):
    placed = (
        P(("blk", "head"), None),
        P(("blk", "head"), None),
        P(("blk", "head"), None),
        P(),
        P(),
    )
    return jax.shard_map(
        local, mesh=mesh, in_specs=placed, out_specs=P(("blk", "head"), None), check_vma=False
    )
```

```python
import functools

import jax
import jax.numpy as jnp
from jax import lax
from jax.experimental import pallas as pl
from jax.experimental.pallas import tpu as pltpu
from jax.sharding import PartitionSpec as P

HD = 128
BLOCK = 512
MAXB = 6


def from_behind(value, axis, steps):
    count = lax.axis_size(axis)
    pairs = [(source, (source + steps) % count) for source in range(count)]
    return lax.ppermute(value, axis, pairs)


def attention_kernel(idx_ref, cnt_ref, q_ref, *refs):
    slabs, (o_ref, k_scr, v_scr, s_scr, m_scr, l_scr, acc_scr, sem) = refs[:6], refs[6:]
    b = pl.program_id(0)
    width = q_ref.shape[1]
    blocks = k_scr.shape[0] // 3

    @pl.when(b == 0)
    def _load_context():
        copies = []
        for i, slab in enumerate(slabs):
            part, half = (1, 0, 2)[i // 2], i % 2
            for column, dst in ((0, k_scr), (width, v_scr)):
                copy = pltpu.make_async_copy(
                    slab.at[:, :, pl.ds(column, width)],
                    dst.at[pl.ds(part * blocks, blocks), half],
                    sem.at[2 * i + column // width],
                )
                copy.start()
                copies.append(copy)
        for copy in copies:
            copy.wait()

    scale = HD ** (-0.5)
    amount = cnt_ref[b]
    m_scr[...] = jnp.full(m_scr.shape, -jnp.inf, jnp.float32)
    for j in range(MAXB):
        @pl.when(j < amount)
        def _scores():
            key_block = k_scr[idx_ref[b * MAXB + j]].reshape(BLOCK, HD)
            scores = lax.dot_general(
                key_block, q_ref[...], (((1,), (1,)), ((), ())),
                preferred_element_type=jnp.float32,
            ) * scale
            s_scr[j] = scores
            m_scr[...] = jnp.maximum(m_scr[...], jnp.max(scores, axis=0, keepdims=True))

    l_scr[...] = jnp.zeros(l_scr.shape, jnp.float32)
    acc_scr[...] = jnp.zeros(acc_scr.shape, jnp.float32)
    for j in range(MAXB):
        @pl.when(j < amount)
        def _mix():
            value_block = v_scr[idx_ref[b * MAXB + j]].reshape(BLOCK, HD)
            expo = jnp.exp(s_scr[j] - m_scr[...])
            l_scr[...] += jnp.sum(expo, axis=0, keepdims=True)
            acc_scr[...] += lax.dot_general(
                value_block, expo.astype(jnp.bfloat16), (((0,), (0,)), ((), ())),
                preferred_element_type=jnp.float32,
            )

    o_ref[...] = jnp.transpose(acc_scr[...] / l_scr[...]).astype(o_ref.dtype)


def attend(query_rows, kv_parts, local_index, count_rows):
    rows, width = query_rows.shape
    blocks_here = rows // BLOCK
    shard_rows = rows
    flops = blocks_here * MAXB * BLOCK * BLOCK * width * 4
    cost = pl.CostEstimate(
        flops=flops,
        transcendentals=blocks_here * MAXB * BLOCK * BLOCK,
        bytes_accessed=(2 + 6) * rows * width * 2,
    )
    any_spec = pl.BlockSpec(memory_space=pl.ANY)
    grid_spec = pltpu.PrefetchScalarGridSpec(
        num_scalar_prefetch=2,
        grid=(blocks_here,),
        in_specs=[pl.BlockSpec((BLOCK, width), lambda b, idx, cnt: (b, 0))] + [any_spec] * 6,
        out_specs=pl.BlockSpec((BLOCK, width), lambda b, idx, cnt: (b, 0)),
        scratch_shapes=[
            pltpu.VMEM((3 * blocks_here, 2, BLOCK // 2, width), jnp.bfloat16),
            pltpu.VMEM((3 * blocks_here, 2, BLOCK // 2, width), jnp.bfloat16),
            pltpu.VMEM((MAXB, BLOCK, BLOCK), jnp.float32),
            pltpu.VMEM((1, BLOCK), jnp.float32),
            pltpu.VMEM((1, BLOCK), jnp.float32),
            pltpu.VMEM((width, BLOCK), jnp.float32),
            pltpu.SemaphoreType.DMA((12,)),
        ],
    )
    return pl.pallas_call(
        attention_kernel,
        out_shape=jax.ShapeDtypeStruct((rows, width), jnp.bfloat16),
        grid_spec=grid_spec,
        compiler_params=pltpu.CompilerParams(dimension_semantics=("arbitrary",)),
        cost_estimate=cost,
    )(local_index, count_rows, query_rows, *kv_parts)


def local(queries, keys, values, key_blocks, counts):
    cycle_size = lax.axis_size("blk")

    def to_heads(x):
        return lax.all_to_all(x, "head", split_axis=1, concat_axis=0, tiled=True)

    rows, model = keys.shape
    heads = model // HD
    paired = jnp.stack(
        [keys.reshape(rows, heads, HD), values.reshape(rows, heads, HD)], axis=2
    ).reshape(rows, 2 * model)
    half = rows // 2
    query_pairs = queries.reshape(half, 2, heads, HD).transpose(0, 2, 1, 3)
    with_queries = jnp.concatenate(
        [paired[half:].reshape(half, heads, 2 * HD), query_pairs.reshape(half, heads, 2 * HD)], axis=2
    ).reshape(half, 4 * model)
    kv_parts = []
    tie = None
    for piece in (paired[:half], with_queries):
        kv_rows = to_heads(piece)
        if tie is not None:
            query_rows = kv_rows[:, 2 * HD:].reshape(2 * kv_rows.shape[0], HD)
            kv_rows = kv_rows[:, :2 * HD] + tie
        earlier, later = from_behind(kv_rows, "blk", 1), from_behind(kv_rows, "blk", -1)
        tie = ((earlier[0, 0] + later[0, 0]) * 0).astype(kv_rows.dtype)
        kv_parts.append((kv_rows, earlier, later))
    slab_shape = (lax.axis_size("head") * half // (BLOCK // 2), BLOCK // 2, 2 * HD)
    kv_parts = [kv_parts[h][p].reshape(slab_shape) for p in range(3) for h in range(2)]
    blocks_here = query_rows.shape[0] // BLOCK
    total_blocks = blocks_here * cycle_size
    first_block = lax.axis_index("blk") * blocks_here
    listed_rows = lax.dynamic_slice_in_dim(key_blocks, first_block, blocks_here, 0)
    count_rows = lax.dynamic_slice_in_dim(counts, first_block, blocks_here, 0)
    local_index = jnp.mod(listed_rows - first_block + blocks_here, total_blocks)
    local_index = jnp.clip(local_index, 0, 3 * blocks_here - 1).reshape(-1)
    attended_rows = attend(query_rows, kv_parts, local_index, count_rows)
    return lax.all_to_all(attended_rows, "head", split_axis=0, concat_axis=1, tiled=True)


def solution(mesh):
    placed = (
        P(("blk", "head"), None),
        P(("blk", "head"), None),
        P(("blk", "head"), None),
        P(),
        P(),
    )
    return jax.shard_map(
        local, mesh=mesh, in_specs=placed, out_specs=P(("blk", "head"), None), check_vma=False
    )
```

```python
import functools

import jax
import jax.numpy as jnp
from jax import lax
from jax.experimental import pallas as pl
from jax.experimental.pallas import tpu as pltpu
from jax.sharding import PartitionSpec as P

HD = 128
BLOCK = 512
MAXB = 6


def from_behind(value, axis, steps):
    count = lax.axis_size(axis)
    pairs = [(source, (source + steps) % count) for source in range(count)]
    return lax.ppermute(value, axis, pairs)


def attention_kernel(idx_ref, cnt_ref, q_ref, *refs):
    slabs, (o_ref, k_scr, v_scr, s_scr, m_scr, l_scr, acc_scr, sem) = refs[:6], refs[6:]
    b = pl.program_id(0)
    width = q_ref.shape[1]
    blocks = k_scr.shape[0] // 3

    @pl.when(b == 0)
    def _load_context():
        copies = []
        for i, slab in enumerate(slabs):
            part, half = (1, 0, 2)[i // 2], i % 2
            for kind, dst in ((0, k_scr), (1, v_scr)):
                copy = pltpu.make_async_copy(
                    slab.at[:, :, kind],
                    dst.at[pl.ds(part * blocks, blocks), half],
                    sem.at[2 * i + kind],
                )
                copy.start()
                copies.append(copy)
        for copy in copies:
            copy.wait()

    scale = HD ** (-0.5)
    amount = cnt_ref[b]
    m_scr[...] = jnp.full(m_scr.shape, -jnp.inf, jnp.float32)
    for j in range(MAXB):
        @pl.when(j < amount)
        def _scores():
            key_block = k_scr[idx_ref[b * MAXB + j]].reshape(BLOCK, HD)
            scores = lax.dot_general(
                key_block, q_ref[...], (((1,), (1,)), ((), ())),
                preferred_element_type=jnp.float32,
            ) * scale
            s_scr[j] = scores
            m_scr[...] = jnp.maximum(m_scr[...], jnp.max(scores, axis=0, keepdims=True))

    l_scr[...] = jnp.zeros(l_scr.shape, jnp.float32)
    acc_scr[...] = jnp.zeros(acc_scr.shape, jnp.float32)
    for j in range(MAXB):
        @pl.when(j < amount)
        def _mix():
            value_block = v_scr[idx_ref[b * MAXB + j]].reshape(BLOCK, HD)
            expo = jnp.exp(s_scr[j] - m_scr[...])
            l_scr[...] += jnp.sum(expo, axis=0, keepdims=True)
            acc_scr[...] += lax.dot_general(
                value_block, expo.astype(jnp.bfloat16), (((0,), (0,)), ((), ())),
                preferred_element_type=jnp.float32,
            )

    o_ref[...] = jnp.transpose(acc_scr[...] / l_scr[...]).astype(o_ref.dtype)


def attend(query_rows, kv_parts, local_index, count_rows):
    rows, width = query_rows.shape
    blocks_here = rows // BLOCK
    _, devs, _, part_rows, _ = kv_parts[0].shape
    shard_rows = rows
    flops = blocks_here * MAXB * BLOCK * BLOCK * width * 4
    cost = pl.CostEstimate(
        flops=flops,
        transcendentals=blocks_here * MAXB * BLOCK * BLOCK,
        bytes_accessed=(2 + 6) * rows * width * 2,
    )
    any_spec = pl.BlockSpec(memory_space=pl.ANY)
    grid_spec = pltpu.PrefetchScalarGridSpec(
        num_scalar_prefetch=2,
        grid=(blocks_here,),
        in_specs=[pl.BlockSpec((BLOCK, width), lambda b, idx, cnt: (b, 0))] + [any_spec] * 6,
        out_specs=pl.BlockSpec((BLOCK, width), lambda b, idx, cnt: (b, 0)),
        scratch_shapes=[
            pltpu.VMEM((3 * blocks_here, 2, devs, part_rows, width), jnp.bfloat16),
            pltpu.VMEM((3 * blocks_here, 2, devs, part_rows, width), jnp.bfloat16),
            pltpu.VMEM((MAXB, BLOCK, BLOCK), jnp.float32),
            pltpu.VMEM((1, BLOCK), jnp.float32),
            pltpu.VMEM((1, BLOCK), jnp.float32),
            pltpu.VMEM((width, BLOCK), jnp.float32),
            pltpu.SemaphoreType.DMA((12,)),
        ],
    )
    return pl.pallas_call(
        attention_kernel,
        out_shape=jax.ShapeDtypeStruct((rows, width), jnp.bfloat16),
        grid_spec=grid_spec,
        compiler_params=pltpu.CompilerParams(dimension_semantics=("arbitrary",)),
        cost_estimate=cost,
    )(local_index, count_rows, query_rows, *kv_parts)


def local(queries, keys, values, key_blocks, counts):
    cycle_size = lax.axis_size("blk")

    def to_heads(x):
        return lax.all_to_all(x, "head", split_axis=1, concat_axis=0, tiled=True)

    rows = keys.shape[0]
    half = rows // 2
    kv_parts = []
    tie = None
    for start in (0, half):
        kv_rows = to_heads(jnp.concatenate([keys[start:start + half], values[start:start + half]], axis=0))
        if tie is not None:
            kv_rows = kv_rows + tie
        earlier, later = from_behind(kv_rows, "blk", 1), from_behind(kv_rows, "blk", -1)
        tie = ((earlier[0, 0] + later[0, 0]) * 0).astype(kv_rows.dtype)
        kv_parts.append((kv_rows, earlier, later))
    query_rows = to_heads(queries)
    devs = BLOCK // rows
    slab_shape = (lax.axis_size("head") // devs, devs, 2, half, HD)
    kv_parts = [kv_parts[h][p].reshape(slab_shape) for p in range(3) for h in range(2)]
    blocks_here = query_rows.shape[0] // BLOCK
    total_blocks = blocks_here * cycle_size
    first_block = lax.axis_index("blk") * blocks_here
    listed_rows = lax.dynamic_slice_in_dim(key_blocks, first_block, blocks_here, 0)
    count_rows = lax.dynamic_slice_in_dim(counts, first_block, blocks_here, 0)
    local_index = jnp.mod(listed_rows - first_block + blocks_here, total_blocks)
    local_index = jnp.clip(local_index, 0, 3 * blocks_here - 1).reshape(-1)
    attended_rows = attend(query_rows, kv_parts, local_index, count_rows)
    return lax.all_to_all(attended_rows, "head", split_axis=0, concat_axis=1, tiled=True)


def solution(mesh):
    placed = (
        P(("blk", "head"), None),
        P(("blk", "head"), None),
        P(("blk", "head"), None),
        P(),
        P(),
    )
    return jax.shard_map(
        local, mesh=mesh, in_specs=placed, out_specs=P(("blk", "head"), None), check_vma=False
    )
```

```python
import functools

import jax
import jax.numpy as jnp
from jax import lax
from jax.experimental import pallas as pl
from jax.experimental.pallas import tpu as pltpu
from jax.sharding import PartitionSpec as P

HD = 128
BLOCK = 512
MAXB = 6


def from_behind(value, axis, steps):
    count = lax.axis_size(axis)
    pairs = [(source, (source + steps) % count) for source in range(count)]
    return lax.ppermute(value, axis, pairs)


def attention_kernel(idx_ref, cnt_ref, q_ref, *refs):
    slabs, (o_ref, k_scr, v_scr, s_scr, m_scr, l_scr, acc_scr, sem) = refs[:6], refs[6:]
    b = pl.program_id(0)
    width = q_ref.shape[1]
    blocks = k_scr.shape[0] // 3

    @pl.when(b == 0)
    def _load_context():
        copies = []
        for i, slab in enumerate(slabs):
            part, half = (1, 0, 2)[i // 2], i % 2
            for kind, dst in ((0, k_scr), (1, v_scr)):
                copy = pltpu.make_async_copy(
                    slab.at[:, :, kind],
                    dst.at[pl.ds(part * blocks, blocks), half],
                    sem.at[2 * i + kind],
                )
                copy.start()
                copies.append(copy)
        for copy in copies:
            copy.wait()

    scale = HD ** (-0.5)
    amount = cnt_ref[b]
    m_scr[...] = jnp.full(m_scr.shape, -jnp.inf, jnp.float32)
    for j in range(MAXB):
        @pl.when(j < amount)
        def _scores():
            key_block = k_scr[idx_ref[b * MAXB + j]].reshape(BLOCK, HD)
            scores = lax.dot_general(
                key_block, q_ref[...], (((1,), (1,)), ((), ())),
                preferred_element_type=jnp.float32,
            ) * scale
            s_scr[j] = scores
            m_scr[...] = jnp.maximum(m_scr[...], jnp.max(scores, axis=0, keepdims=True))

    l_scr[...] = jnp.zeros(l_scr.shape, jnp.float32)
    acc_scr[...] = jnp.zeros(acc_scr.shape, jnp.float32)
    for j in range(MAXB):
        @pl.when(j < amount)
        def _mix():
            value_block = v_scr[idx_ref[b * MAXB + j]].reshape(BLOCK, HD)
            expo = jnp.exp(s_scr[j] - m_scr[...])
            l_scr[...] += jnp.sum(expo, axis=0, keepdims=True)
            acc_scr[...] += lax.dot_general(
                value_block, expo.astype(jnp.bfloat16), (((0,), (0,)), ((), ())),
                preferred_element_type=jnp.float32,
            )

    o_ref[...] = jnp.transpose(acc_scr[...] / l_scr[...]).astype(o_ref.dtype)


def attend(query_rows, kv_parts, local_index, count_rows):
    rows, width = query_rows.shape
    blocks_here = rows // BLOCK
    _, devs, _, part_rows, _ = kv_parts[0].shape
    shard_rows = rows
    flops = blocks_here * MAXB * BLOCK * BLOCK * width * 4
    cost = pl.CostEstimate(
        flops=flops,
        transcendentals=blocks_here * MAXB * BLOCK * BLOCK,
        bytes_accessed=(2 + 6) * rows * width * 2,
    )
    any_spec = pl.BlockSpec(memory_space=pl.ANY)
    grid_spec = pltpu.PrefetchScalarGridSpec(
        num_scalar_prefetch=2,
        grid=(blocks_here,),
        in_specs=[pl.BlockSpec((BLOCK, width), lambda b, idx, cnt: (b, 0))] + [any_spec] * 6,
        out_specs=pl.BlockSpec((BLOCK, width), lambda b, idx, cnt: (b, 0)),
        scratch_shapes=[
            pltpu.VMEM((3 * blocks_here, 2, devs, part_rows, width), jnp.bfloat16),
            pltpu.VMEM((3 * blocks_here, 2, devs, part_rows, width), jnp.bfloat16),
            pltpu.VMEM((MAXB, BLOCK, BLOCK), jnp.float32),
            pltpu.VMEM((1, BLOCK), jnp.float32),
            pltpu.VMEM((1, BLOCK), jnp.float32),
            pltpu.VMEM((width, BLOCK), jnp.float32),
            pltpu.SemaphoreType.DMA((12,)),
        ],
    )
    return pl.pallas_call(
        attention_kernel,
        out_shape=jax.ShapeDtypeStruct((rows, width), jnp.bfloat16),
        grid_spec=grid_spec,
        compiler_params=pltpu.CompilerParams(dimension_semantics=("arbitrary",)),
        cost_estimate=cost,
    )(local_index, count_rows, query_rows, *kv_parts)


def local(queries, keys, values, key_blocks, counts):
    cycle_size = lax.axis_size("blk")

    def to_heads(x):
        return lax.all_to_all(x, "head", split_axis=1, concat_axis=0, tiled=True)

    rows = keys.shape[0]
    half = rows // 2
    kv_parts = []
    for start in (0, half):
        kv_rows = to_heads(jnp.concatenate([keys[start:start + half], values[start:start + half]], axis=0))
        if kv_parts:
            own, earlier, later = kv_parts[0]
            kv_rows, earlier, later = lax.optimization_barrier((kv_rows, earlier, later))
            kv_parts[0] = (own, earlier, later)
        earlier, later = from_behind(kv_rows, "blk", 1), from_behind(kv_rows, "blk", -1)
        kv_parts.append((kv_rows, earlier, later))
    query_rows = to_heads(queries)
    devs = BLOCK // rows
    slab_shape = (lax.axis_size("head") // devs, devs, 2, half, HD)
    kv_parts = [kv_parts[h][p].reshape(slab_shape) for p in range(3) for h in range(2)]
    blocks_here = query_rows.shape[0] // BLOCK
    total_blocks = blocks_here * cycle_size
    first_block = lax.axis_index("blk") * blocks_here
    listed_rows = lax.dynamic_slice_in_dim(key_blocks, first_block, blocks_here, 0)
    count_rows = lax.dynamic_slice_in_dim(counts, first_block, blocks_here, 0)
    local_index = jnp.mod(listed_rows - first_block + blocks_here, total_blocks)
    local_index = jnp.clip(local_index, 0, 3 * blocks_here - 1).reshape(-1)
    attended_rows = attend(query_rows, kv_parts, local_index, count_rows)
    return lax.all_to_all(attended_rows, "head", split_axis=0, concat_axis=1, tiled=True)


def solution(mesh):
    placed = (
        P(("blk", "head"), None),
        P(("blk", "head"), None),
        P(("blk", "head"), None),
        P(),
        P(),
    )
    return jax.shard_map(
        local, mesh=mesh, in_specs=placed, out_specs=P(("blk", "head"), None), check_vma=False
    )
```

```python
import functools

import jax
import jax.numpy as jnp
from jax import lax
from jax.experimental import pallas as pl
from jax.experimental.pallas import tpu as pltpu
from jax.sharding import PartitionSpec as P

HD = 128
BLOCK = 512
MAXB = 6
MINB = 3


def from_behind(value, axis, steps):
    count = lax.axis_size(axis)
    pairs = [(source, (source + steps) % count) for source in range(count)]
    return lax.ppermute(value, axis, pairs)


def attention_kernel(idx_ref, cnt_ref, q_ref, *refs):
    slabs, (o_ref, k_scr, v_scr, s_scr, m_scr, l_scr, acc_scr, sem) = refs[:6], refs[6:]
    b = pl.program_id(0)
    width = q_ref.shape[1]
    blocks = k_scr.shape[0] // 3

    @pl.when(b == 0)
    def _load_context():
        copies = []
        for i, slab in enumerate(slabs):
            part, half = (1, 0, 2)[i // 2], i % 2
            for kind, dst in ((0, k_scr), (1, v_scr)):
                copy = pltpu.make_async_copy(
                    slab.at[:, :, kind],
                    dst.at[pl.ds(part * blocks, blocks), half],
                    sem.at[2 * i + kind],
                )
                copy.start()
                copies.append(copy)
        for copy in copies:
            copy.wait()

    scale = HD ** (-0.5)
    amount = cnt_ref[b]
    m_scr[...] = jnp.full(m_scr.shape, -jnp.inf, jnp.float32)
    for j in range(MAXB):
        @pl.when(True if j < MINB else j < amount)
        def _scores():
            key_block = k_scr[idx_ref[b * MAXB + j]].reshape(BLOCK, HD)
            scores = lax.dot_general(
                key_block, q_ref[...], (((1,), (1,)), ((), ())),
                preferred_element_type=jnp.float32,
            ) * scale
            s_scr[j] = scores
            m_scr[...] = jnp.maximum(m_scr[...], jnp.max(scores, axis=0, keepdims=True))

    l_scr[...] = jnp.zeros(l_scr.shape, jnp.float32)
    acc_scr[...] = jnp.zeros(acc_scr.shape, jnp.float32)
    for j in range(MAXB):
        @pl.when(True if j < MINB else j < amount)
        def _mix():
            value_block = v_scr[idx_ref[b * MAXB + j]].reshape(BLOCK, HD)
            expo = jnp.exp(s_scr[j] - m_scr[...])
            l_scr[...] += jnp.sum(expo, axis=0, keepdims=True)
            acc_scr[...] += lax.dot_general(
                value_block, expo.astype(jnp.bfloat16), (((0,), (0,)), ((), ())),
                preferred_element_type=jnp.float32,
            )

    o_ref[...] = jnp.transpose(acc_scr[...] / l_scr[...]).astype(o_ref.dtype)


def attend(query_rows, kv_parts, local_index, count_rows):
    rows, width = query_rows.shape
    blocks_here = rows // BLOCK
    _, devs, _, part_rows, _ = kv_parts[0].shape
    shard_rows = rows
    flops = blocks_here * MAXB * BLOCK * BLOCK * width * 4
    cost = pl.CostEstimate(
        flops=flops,
        transcendentals=blocks_here * MAXB * BLOCK * BLOCK,
        bytes_accessed=(2 + 6) * rows * width * 2,
    )
    any_spec = pl.BlockSpec(memory_space=pl.ANY)
    grid_spec = pltpu.PrefetchScalarGridSpec(
        num_scalar_prefetch=2,
        grid=(blocks_here,),
        in_specs=[pl.BlockSpec((BLOCK, width), lambda b, idx, cnt: (b, 0))] + [any_spec] * 6,
        out_specs=pl.BlockSpec((BLOCK, width), lambda b, idx, cnt: (b, 0)),
        scratch_shapes=[
            pltpu.VMEM((3 * blocks_here, 2, devs, part_rows, width), jnp.bfloat16),
            pltpu.VMEM((3 * blocks_here, 2, devs, part_rows, width), jnp.bfloat16),
            pltpu.VMEM((MAXB, BLOCK, BLOCK), jnp.float32),
            pltpu.VMEM((1, BLOCK), jnp.float32),
            pltpu.VMEM((1, BLOCK), jnp.float32),
            pltpu.VMEM((width, BLOCK), jnp.float32),
            pltpu.SemaphoreType.DMA((12,)),
        ],
    )
    return pl.pallas_call(
        attention_kernel,
        out_shape=jax.ShapeDtypeStruct((rows, width), jnp.bfloat16),
        grid_spec=grid_spec,
        compiler_params=pltpu.CompilerParams(dimension_semantics=("arbitrary",)),
        cost_estimate=cost,
    )(local_index, count_rows, query_rows, *kv_parts)


def local(queries, keys, values, key_blocks, counts):
    cycle_size = lax.axis_size("blk")

    def to_heads(x):
        return lax.all_to_all(x, "head", split_axis=1, concat_axis=0, tiled=True)

    rows = keys.shape[0]
    half = rows // 2
    kv_parts = []
    tie = None
    for start in (0, half):
        kv_rows = to_heads(jnp.concatenate([keys[start:start + half], values[start:start + half]], axis=0))
        if tie is not None:
            kv_rows = kv_rows + tie
        earlier, later = from_behind(kv_rows, "blk", 1), from_behind(kv_rows, "blk", -1)
        tie = ((earlier[0, 0] + later[0, 0]) * 0).astype(kv_rows.dtype)
        kv_parts.append((kv_rows, earlier, later))
    query_rows = to_heads(queries)
    devs = BLOCK // rows
    slab_shape = (lax.axis_size("head") // devs, devs, 2, half, HD)
    kv_parts = [kv_parts[h][p].reshape(slab_shape) for p in range(3) for h in range(2)]
    blocks_here = query_rows.shape[0] // BLOCK
    total_blocks = blocks_here * cycle_size
    first_block = lax.axis_index("blk") * blocks_here
    listed_rows = lax.dynamic_slice_in_dim(key_blocks, first_block, blocks_here, 0)
    count_rows = lax.dynamic_slice_in_dim(counts, first_block, blocks_here, 0)
    local_index = jnp.mod(listed_rows - first_block + blocks_here, total_blocks)
    local_index = jnp.clip(local_index, 0, 3 * blocks_here - 1).reshape(-1)
    attended_rows = attend(query_rows, kv_parts, local_index, count_rows)
    return lax.all_to_all(attended_rows, "head", split_axis=0, concat_axis=1, tiled=True)


def solution(mesh):
    placed = (
        P(("blk", "head"), None),
        P(("blk", "head"), None),
        P(("blk", "head"), None),
        P(),
        P(),
    )
    return jax.shard_map(
        local, mesh=mesh, in_specs=placed, out_specs=P(("blk", "head"), None), check_vma=False
    )
```

```python
import functools

import jax
import jax.numpy as jnp
from jax import lax
from jax.experimental import pallas as pl
from jax.experimental.pallas import tpu as pltpu
from jax.sharding import PartitionSpec as P

HD = 128
BLOCK = 512
MAXB = 6
MINB = 3


def from_behind(value, axis, steps):
    count = lax.axis_size(axis)
    pairs = [(source, (source + steps) % count) for source in range(count)]
    return lax.ppermute(value, axis, pairs)


def attention_kernel(idx_ref, cnt_ref, q_ref, *refs):
    slabs, (o_ref, k_scr, v_scr, s_scr, m_scr, l_scr, acc_scr, sem) = refs[:6], refs[6:]
    b = pl.program_id(0)
    width = q_ref.shape[1]
    blocks = k_scr.shape[0] // 3

    @pl.when(b == 0)
    def _load_context():
        copies = []
        for i, slab in enumerate(slabs):
            part, half = (1, 0, 2)[i // 2], i % 2
            for kind, dst in ((0, k_scr), (1, v_scr)):
                copy = pltpu.make_async_copy(
                    slab.at[:, :, kind],
                    dst.at[pl.ds(part * blocks, blocks), half],
                    sem.at[2 * i + kind],
                )
                copy.start()
                copies.append(copy)
        for copy in copies:
            copy.wait()

    scale = HD ** (-0.5)
    amount = cnt_ref[b]
    amount = jnp.clip(amount, MINB, MAXB)
    for used in range(MINB, MAXB + 1):
        @pl.when(amount == used)
        def _attend():
            m_scr[...] = jnp.full(m_scr.shape, -jnp.inf, jnp.float32)
            for j in range(used):
                @pl.when(True)
                def _scores():
                    key_block = k_scr[idx_ref[b * MAXB + j]].reshape(BLOCK, HD)
                    scores = lax.dot_general(
                        key_block, q_ref[...], (((1,), (1,)), ((), ())),
                        preferred_element_type=jnp.float32,
                    ) * scale
                    s_scr[j] = scores
                    m_scr[...] = jnp.maximum(m_scr[...], jnp.max(scores, axis=0, keepdims=True))

            l_scr[...] = jnp.zeros(l_scr.shape, jnp.float32)
            acc_scr[...] = jnp.zeros(acc_scr.shape, jnp.float32)
            for j in range(used):
                @pl.when(True)
                def _mix():
                    value_block = v_scr[idx_ref[b * MAXB + j]].reshape(BLOCK, HD)
                    expo = jnp.exp(s_scr[j] - m_scr[...])
                    l_scr[...] += jnp.sum(expo, axis=0, keepdims=True)
                    acc_scr[...] += lax.dot_general(
                        value_block, expo.astype(jnp.bfloat16), (((0,), (0,)), ((), ())),
                        preferred_element_type=jnp.float32,
                    )


    o_ref[...] = jnp.transpose(acc_scr[...] / l_scr[...]).astype(o_ref.dtype)


def attend(query_rows, kv_parts, local_index, count_rows):
    rows, width = query_rows.shape
    blocks_here = rows // BLOCK
    _, devs, _, part_rows, _ = kv_parts[0].shape
    shard_rows = rows
    flops = blocks_here * MAXB * BLOCK * BLOCK * width * 4
    cost = pl.CostEstimate(
        flops=flops,
        transcendentals=blocks_here * MAXB * BLOCK * BLOCK,
        bytes_accessed=(2 + 6) * rows * width * 2,
    )
    any_spec = pl.BlockSpec(memory_space=pl.ANY)
    grid_spec = pltpu.PrefetchScalarGridSpec(
        num_scalar_prefetch=2,
        grid=(blocks_here,),
        in_specs=[pl.BlockSpec((BLOCK, width), lambda b, idx, cnt: (b, 0))] + [any_spec] * 6,
        out_specs=pl.BlockSpec((BLOCK, width), lambda b, idx, cnt: (b, 0)),
        scratch_shapes=[
            pltpu.VMEM((3 * blocks_here, 2, devs, part_rows, width), jnp.bfloat16),
            pltpu.VMEM((3 * blocks_here, 2, devs, part_rows, width), jnp.bfloat16),
            pltpu.VMEM((MAXB, BLOCK, BLOCK), jnp.float32),
            pltpu.VMEM((1, BLOCK), jnp.float32),
            pltpu.VMEM((1, BLOCK), jnp.float32),
            pltpu.VMEM((width, BLOCK), jnp.float32),
            pltpu.SemaphoreType.DMA((12,)),
        ],
    )
    return pl.pallas_call(
        attention_kernel,
        out_shape=jax.ShapeDtypeStruct((rows, width), jnp.bfloat16),
        grid_spec=grid_spec,
        compiler_params=pltpu.CompilerParams(dimension_semantics=("arbitrary",)),
        cost_estimate=cost,
    )(local_index, count_rows, query_rows, *kv_parts)


def local(queries, keys, values, key_blocks, counts):
    cycle_size = lax.axis_size("blk")

    def to_heads(x):
        return lax.all_to_all(x, "head", split_axis=1, concat_axis=0, tiled=True)

    rows = keys.shape[0]
    half = rows // 2
    kv_parts = []
    tie = None
    for start in (0, half):
        kv_rows = to_heads(jnp.concatenate([keys[start:start + half], values[start:start + half]], axis=0))
        if tie is not None:
            kv_rows = kv_rows + tie
        earlier, later = from_behind(kv_rows, "blk", 1), from_behind(kv_rows, "blk", -1)
        tie = ((earlier[0, 0] + later[0, 0]) * 0).astype(kv_rows.dtype)
        kv_parts.append((kv_rows, earlier, later))
    query_rows = to_heads(queries)
    devs = BLOCK // rows
    slab_shape = (lax.axis_size("head") // devs, devs, 2, half, HD)
    kv_parts = [kv_parts[h][p].reshape(slab_shape) for p in range(3) for h in range(2)]
    blocks_here = query_rows.shape[0] // BLOCK
    total_blocks = blocks_here * cycle_size
    first_block = lax.axis_index("blk") * blocks_here
    listed_rows = lax.dynamic_slice_in_dim(key_blocks, first_block, blocks_here, 0)
    count_rows = lax.dynamic_slice_in_dim(counts, first_block, blocks_here, 0)
    local_index = jnp.mod(listed_rows - first_block + blocks_here, total_blocks)
    local_index = jnp.clip(local_index, 0, 3 * blocks_here - 1).reshape(-1)
    attended_rows = attend(query_rows, kv_parts, local_index, count_rows)
    return lax.all_to_all(attended_rows, "head", split_axis=0, concat_axis=1, tiled=True)


def solution(mesh):
    placed = (
        P(("blk", "head"), None),
        P(("blk", "head"), None),
        P(("blk", "head"), None),
        P(),
        P(),
    )
    return jax.shard_map(
        local, mesh=mesh, in_specs=placed, out_specs=P(("blk", "head"), None), check_vma=False
    )
```

```python
import functools

import jax
import jax.numpy as jnp
from jax import lax
from jax.experimental import pallas as pl
from jax.experimental.pallas import tpu as pltpu
from jax.sharding import PartitionSpec as P

HD = 128
BLOCK = 512
MAXB = 6
MINB = 3


def from_behind(value, axis, steps):
    count = lax.axis_size(axis)
    pairs = [(source, (source + steps) % count) for source in range(count)]
    return lax.ppermute(value, axis, pairs)


def attention_kernel(idx_ref, cnt_ref, q_ref, *refs):
    slabs, (o_ref, k_scr, v_scr, s_scr, m_scr, l_scr, acc_scr, sem) = refs[:6], refs[6:]
    b = pl.program_id(0)
    width = q_ref.shape[1]
    blocks = k_scr.shape[0] // 3

    @pl.when(b == 0)
    def _load_context():
        copies = []
        for i, slab in enumerate(slabs):
            part, half = (1, 0, 2)[i // 2], i % 2
            for kind, dst in ((0, k_scr), (1, v_scr)):
                copy = pltpu.make_async_copy(
                    slab.at[:, :, kind],
                    dst.at[pl.ds(part * blocks, blocks), half],
                    sem.at[2 * i + kind],
                )
                copy.start()
                copies.append(copy)
        for copy in copies:
            copy.wait()

    scale = HD ** (-0.5)
    amount = cnt_ref[b]
    amount = jnp.clip(amount, MINB, MAXB)
    for used in range(MINB, MAXB + 1):
        @pl.when(amount == used)
        def _attend():
            top = jnp.full(m_scr.shape, -jnp.inf, jnp.float32)
            for j in range(used):
                key_block = k_scr[idx_ref[b * MAXB + j]].reshape(BLOCK, HD)
                scores = lax.dot_general(
                    key_block, q_ref[...], (((1,), (1,)), ((), ())),
                    preferred_element_type=jnp.float32,
                ) * scale
                s_scr[j] = scores
                top = jnp.maximum(top, jnp.max(scores, axis=0, keepdims=True))
            total = jnp.zeros(l_scr.shape, jnp.float32)
            mixed = jnp.zeros(acc_scr.shape, jnp.float32)
            for j in range(used):
                value_block = v_scr[idx_ref[b * MAXB + j]].reshape(BLOCK, HD)
                expo = jnp.exp(s_scr[j] - top)
                total = total + jnp.sum(expo, axis=0, keepdims=True)
                mixed = mixed + lax.dot_general(
                    value_block, expo.astype(jnp.bfloat16), (((0,), (0,)), ((), ())),
                    preferred_element_type=jnp.float32,
                )
            o_ref[...] = jnp.transpose(mixed / total).astype(o_ref.dtype)


def attend(query_rows, kv_parts, local_index, count_rows):
    rows, width = query_rows.shape
    blocks_here = rows // BLOCK
    _, devs, _, part_rows, _ = kv_parts[0].shape
    shard_rows = rows
    flops = blocks_here * MAXB * BLOCK * BLOCK * width * 4
    cost = pl.CostEstimate(
        flops=flops,
        transcendentals=blocks_here * MAXB * BLOCK * BLOCK,
        bytes_accessed=(2 + 6) * rows * width * 2,
    )
    any_spec = pl.BlockSpec(memory_space=pl.ANY)
    grid_spec = pltpu.PrefetchScalarGridSpec(
        num_scalar_prefetch=2,
        grid=(blocks_here,),
        in_specs=[pl.BlockSpec((BLOCK, width), lambda b, idx, cnt: (b, 0))] + [any_spec] * 6,
        out_specs=pl.BlockSpec((BLOCK, width), lambda b, idx, cnt: (b, 0)),
        scratch_shapes=[
            pltpu.VMEM((3 * blocks_here, 2, devs, part_rows, width), jnp.bfloat16),
            pltpu.VMEM((3 * blocks_here, 2, devs, part_rows, width), jnp.bfloat16),
            pltpu.VMEM((MAXB, BLOCK, BLOCK), jnp.float32),
            pltpu.VMEM((1, BLOCK), jnp.float32),
            pltpu.VMEM((1, BLOCK), jnp.float32),
            pltpu.VMEM((width, BLOCK), jnp.float32),
            pltpu.SemaphoreType.DMA((12,)),
        ],
    )
    return pl.pallas_call(
        attention_kernel,
        out_shape=jax.ShapeDtypeStruct((rows, width), jnp.bfloat16),
        grid_spec=grid_spec,
        compiler_params=pltpu.CompilerParams(dimension_semantics=("arbitrary",)),
        cost_estimate=cost,
    )(local_index, count_rows, query_rows, *kv_parts)


def local(queries, keys, values, key_blocks, counts):
    cycle_size = lax.axis_size("blk")

    def to_heads(x):
        return lax.all_to_all(x, "head", split_axis=1, concat_axis=0, tiled=True)

    rows = keys.shape[0]
    half = rows // 2
    kv_parts = []
    tie = None
    for start in (0, half):
        kv_rows = to_heads(jnp.concatenate([keys[start:start + half], values[start:start + half]], axis=0))
        if tie is not None:
            kv_rows = kv_rows + tie
        earlier, later = from_behind(kv_rows, "blk", 1), from_behind(kv_rows, "blk", -1)
        tie = ((earlier[0, 0] + later[0, 0]) * 0).astype(kv_rows.dtype)
        kv_parts.append((kv_rows, earlier, later))
    query_rows = to_heads(queries)
    devs = BLOCK // rows
    slab_shape = (lax.axis_size("head") // devs, devs, 2, half, HD)
    kv_parts = [kv_parts[h][p].reshape(slab_shape) for p in range(3) for h in range(2)]
    blocks_here = query_rows.shape[0] // BLOCK
    total_blocks = blocks_here * cycle_size
    first_block = lax.axis_index("blk") * blocks_here
    listed_rows = lax.dynamic_slice_in_dim(key_blocks, first_block, blocks_here, 0)
    count_rows = lax.dynamic_slice_in_dim(counts, first_block, blocks_here, 0)
    local_index = jnp.mod(listed_rows - first_block + blocks_here, total_blocks)
    local_index = jnp.clip(local_index, 0, 3 * blocks_here - 1).reshape(-1)
    attended_rows = attend(query_rows, kv_parts, local_index, count_rows)
    return lax.all_to_all(attended_rows, "head", split_axis=0, concat_axis=1, tiled=True)


def solution(mesh):
    placed = (
        P(("blk", "head"), None),
        P(("blk", "head"), None),
        P(("blk", "head"), None),
        P(),
        P(),
    )
    return jax.shard_map(
        local, mesh=mesh, in_specs=placed, out_specs=P(("blk", "head"), None), check_vma=False
    )
```
